32 devices in a mesh: dp: 4 (over y, core), seq: 8 (over z, x).
Axes of the slice: x: 2, y: 2, z: 4, core: 2. Of those that a mesh axis runs over, the one named last changes fastest.
Arguments:
- inputs: bfloat16 [4, 1024, 2048], P('dp', 'seq'), may hold values from -6 to 6
- w_query: bfloat16 [2048, 2048], P(None, 'seq'), may hold values from -0.125 to 0.125
- sharpness: float32 [32], P('seq'), may hold values from 0.03 to 0.3
- pattern: int32 [8, 2], replicated, may hold values from 0 to 7, as said below
- lengths: int32 [4], P('dp'), may hold values from 512 to 1024
- probes: bfloat16 [4, 1024, 2048], P('dp', 'seq'), may hold values from -36 to 36
- start_vector: float32 [2048], replicated, may hold values from -6 to 6
Outputs:
- branch: bfloat16 [4, 1024, 2048], P('dp', 'seq')
- probe_vjp: bfloat16 [4, 1024, 2048], P('dp', 'seq')
- logdet_terms: float32 [4, 2], P('dp')
- sharpness_grad: float32 [32], P('seq')
- spec_vector: float32 [2048], replicated
- spec_norm: float32 [1], replicated
The draws below stay inside these ranges and needn't reach their ends.
Inputs may be any that keep to these rules, and one draw needn't show every extreme that they name: `pattern`: entry 0 of row I is I itself; the 2 entries of a row differ.
All inputs are finite; a program needn't handle non-finite values.
Results may differ from the reference program's by a relative error of at most 0.007.
Values may be sent and summed in bfloat16 or wider, within the bound.
A program may use at most 64 MiB of HBM per device.

```python
import math
import jax
import jax.numpy as jnp
from jax import lax

D = 2048
HEADS = 32
BLOCK = 128
NB = 2
SEQ_LEN = 1024
SEQS = 4
INNER = 2048


def draw_pattern(key, part):
    block_count = SEQ_LEN // BLOCK
    scores = jax.random.randint(key, (block_count, block_count - 1), 0, 1 << 20) * (block_count - 1)
    scores = scores + jnp.arange(block_count - 1, dtype=jnp.int32)[None, :]
    order = jnp.argsort(scores, axis=1, stable=True)
    offsets = order[:, :NB - 1] + 1
    own_block = jnp.arange(block_count, dtype=jnp.int32)[:, None]
    others = (own_block + offsets) % block_count
    return jnp.concatenate([own_block, others.astype(jnp.int32)], axis=1).astype(jnp.int32)


def draw_lengths(key, part):
    key_a = jax.random.fold_in(key, 11)
    key_b = jax.random.fold_in(key, 12)
    half_len = SEQ_LEN // 2
    drawn = jax.random.randint(key_a, (SEQS,), half_len, SEQ_LEN + 1)
    order = jax.random.permutation(key_b, SEQS)
    drawn = drawn.at[order[0]].set(SEQ_LEN)
    drawn = drawn.at[order[1]].set(half_len)
    return drawn.astype(jnp.int32)


def draw_probes(key, part):
    key_a = jax.random.fold_in(key, 21)
    seq_rise = 1.0 + 2.0 * jnp.arange(SEQS, dtype=jnp.float32) / (SEQS - 1)
    pos_rise = 1.0 + 2.0 * jnp.arange(SEQ_LEN, dtype=jnp.float32) / (SEQ_LEN - 1)
    base = jnp.clip(jax.random.normal(key_a, (SEQS, SEQ_LEN, D), jnp.float32), -4.0, 4.0)
    result = base * seq_rise[:, None, None] * pos_rise[None, :, None]
    return result.astype(jnp.bfloat16)


def levels(rng, dims, shards, least, largest):
    loudness, own = 1.0, jax.random.fold_in(rng, 6)
    for axis_at, shards_of in shards:
        draws = jnp.exp(jax.random.uniform(jax.random.fold_in(own, axis_at), (shards_of,), jnp.float32, least / len(shards), largest / len(shards)))
        loudness = loudness * jnp.repeat(draws, dims[axis_at] // shards_of).reshape([-1 if axis == axis_at else 1 for axis in range(len(dims))])
    return loudness


def normal_values(own_key, extent, width, limit, cuts=(), kind=jnp.bfloat16):
    gain = levels(own_key, extent, cuts, -0.22, 0.18) if cuts else 1.0
    values = jax.random.normal(own_key, extent, jnp.float32) * width * gain
    return jnp.minimum(jnp.maximum(values, -limit), limit).astype(kind)


def setup_inputs(seed: int = 0) -> dict:
    key_list = jax.random.split(jax.random.key(seed), 8)
    inputs = normal_values(key_list[0], (SEQS, SEQ_LEN, D), 1.0, 6.0, ((0, 4), (1, 8)))
    w_query = normal_values(key_list[1], (D, INNER), D ** -0.5, 0.125, ((1, 8),))
    sharpness = jnp.clip(jnp.exp(math.log(0.3) - 2.3025852 * jax.random.uniform(key_list[2], (HEADS,), jnp.float32) ** levels(key_list[2], (HEADS,), ((0, 8),), -0.2, 0.2)), 0.03, 0.3)
    pattern = draw_pattern(jax.random.fold_in(key_list[7], 71), 0)
    lengths = draw_lengths(jax.random.fold_in(key_list[7], 71), 0)
    probes = draw_probes(jax.random.fold_in(key_list[7], 71), 0)
    start_vector = normal_values(key_list[6], (D,), 1.0, 6.0, (), jnp.float32)
    return dict(inputs=inputs, w_query=w_query, sharpness=sharpness, pattern=pattern, lengths=lengths, probes=probes, start_vector=start_vector)


def head_forward(query_head, sharp_head, pattern, length):
    head_size, seq_total = query_head.shape
    block_count, fanout = pattern.shape
    block_len = seq_total // block_count
    query_tiles = jnp.transpose(query_head.reshape(head_size, block_count, block_len), (1, 0, 2))
    key_tiles = jnp.take(query_tiles, pattern, axis=0)
    query_norms = lax.optimization_barrier(jnp.sum(jnp.square(query_tiles.astype(jnp.float32)), axis=1))
    key_norms = jnp.take(query_norms, pattern, axis=0)
    inner_dots = jnp.einsum('qdi,qndj->qinj', query_tiles.astype(jnp.float32), key_tiles.astype(jnp.float32))
    distance = query_norms[:, :, None, None] + key_norms[:, None, :, :] - 2.0 * inner_dots
    query_pos = jnp.arange(block_count, dtype=jnp.int32)[:, None] * block_len + jnp.arange(block_len, dtype=jnp.int32)[None, :]
    key_pos = pattern[:, :, None] * block_len + jnp.arange(block_len, dtype=jnp.int32)[None, None, :]
    allowed = (key_pos[:, None, :, :] < length) | (key_pos[:, None, :, :] == query_pos[:, :, None, None])
    factor = sharp_head / math.sqrt(head_size)
    weights = jnp.where(allowed, jnp.exp(-factor * distance), 0.0)
    totals = lax.optimization_barrier(jnp.sum(weights, axis=(2, 3)))
    softmax = weights / totals[:, :, None, None]
    softmax_low = softmax.astype(jnp.bfloat16)
    mixed_out = jnp.einsum('qinj,qndj->qdi', softmax_low.astype(jnp.float32), key_tiles.astype(jnp.float32))
    attended = jnp.transpose(mixed_out, (1, 0, 2)).reshape(head_size, seq_total)
    return (attended, softmax, softmax_low, distance)

def head_backward(query_head, cotangent, softmax, softmax_low, sharp_head, pattern):
    head_size, seq_total = query_head.shape
    block_count, fanout = pattern.shape
    block_len = seq_total // block_count
    query_tiles = jnp.transpose(query_head.reshape(head_size, block_count, block_len), (1, 0, 2))
    key_tiles = jnp.take(query_tiles, pattern, axis=0)
    co_tiles = jnp.transpose(cotangent.reshape(head_size, block_count, block_len), (1, 0, 2))
    prob_grad = jnp.einsum('qdi,qndj->qinj', co_tiles.astype(jnp.float32), key_tiles.astype(jnp.float32))
    row_inner = lax.optimization_barrier(jnp.sum(softmax * prob_grad, axis=(2, 3)))
    score_grad = softmax * (prob_grad - row_inner[:, :, None, None])
    factor = sharp_head / math.sqrt(head_size)
    coefficient = (-2.0 * factor * score_grad).astype(jnp.bfloat16)
    coef_wide = coefficient.astype(jnp.float32)
    row_total = lax.optimization_barrier(jnp.sum(coef_wide, axis=(2, 3)))
    col_total = lax.optimization_barrier(jnp.sum(coef_wide, axis=1))
    query_part = query_tiles.astype(jnp.float32) * row_total[:, None, :] - jnp.einsum('qinj,qndj->qdi', coef_wide, key_tiles.astype(jnp.float32))
    key_part = key_tiles.astype(jnp.float32) * col_total[:, :, None, :] - jnp.einsum('qinj,qdi->qndj', coef_wide, query_tiles.astype(jnp.float32))
    key_part = key_part + jnp.einsum('qinj,qdi->qndj', softmax_low.astype(jnp.float32), co_tiles.astype(jnp.float32))
    selector = (pattern[:, :, None] == jnp.arange(block_count, dtype=jnp.int32)[None, None, :]).astype(jnp.float32)
    spread = jnp.einsum('qnk,qndj->kdj', selector, key_part, precision=lax.Precision.HIGHEST)
    total_grad = jnp.transpose(query_part + spread, (1, 0, 2)).reshape(head_size, seq_total)
    return (total_grad, score_grad)

def reference(inputs, w_query, sharpness, pattern, lengths, probes, start_vector):
    head_count = sharpness.shape[0]
    width_inner = w_query.shape[1]
    head_size = width_inner // head_count
    seq_total = inputs.shape[1]

    def one_sequence(items):
        tokens, probe_rows, length = items
        valid = (jnp.arange(seq_total, dtype=jnp.int32) < length)[:, None]
        masked = jnp.where(valid, probe_rows, jnp.zeros_like(probe_rows))
        queries = jnp.dot(tokens, w_query, preferred_element_type=jnp.float32).astype(jnp.bfloat16).T.reshape(head_count, head_size, seq_total)
        first_cot = jnp.dot(masked, w_query, preferred_element_type=jnp.float32).astype(jnp.bfloat16).T.reshape(head_count, head_size, seq_total)

        def first_pass(head_items):
            query_head, cot_head, sharp_head = head_items
            attended, softmax, softmax_low, distance = head_forward(query_head, sharp_head, pattern, length)
            grad_one, score_grad = head_backward(query_head, cot_head, softmax, softmax_low, sharp_head, pattern)
            sharp_part = jnp.sum(score_grad * distance) * (-1.0 / math.sqrt(head_size))
            return (attended.astype(jnp.bfloat16), grad_one, sharp_part)
        attended, grad_one, sharp_parts = lax.map(first_pass, (queries, first_cot, sharpness))
        term_one = jnp.sum(grad_one * first_cot.astype(jnp.float32))
        att_rows = attended.reshape(width_inner, seq_total).T
        branch = jnp.dot(att_rows, w_query.T, preferred_element_type=jnp.float32).astype(jnp.bfloat16)
        back_rows = grad_one.astype(jnp.bfloat16).reshape(width_inner, seq_total).T
        probe_vjp = jnp.dot(back_rows, w_query.T, preferred_element_type=jnp.float32).astype(jnp.bfloat16)
        second_cot = jnp.dot(probe_vjp, w_query, preferred_element_type=jnp.float32).astype(jnp.bfloat16).T.reshape(head_count, head_size, seq_total)

        def second_pass(head_items):
            query_head, cot_head, sharp_head = head_items
            attended_again, softmax, softmax_low, distance = head_forward(query_head, sharp_head, pattern, length)
            grad_two, score_grad = head_backward(query_head, cot_head, softmax, softmax_low, sharp_head, pattern)
            return grad_two
        grad_two = lax.map(second_pass, (queries, second_cot, sharpness))
        term_two = jnp.sum(grad_two * first_cot.astype(jnp.float32))
        term_vec = jnp.stack([term_one, term_two]) / (length.astype(jnp.float32) * width_inner)
        return (branch, probe_vjp, term_vec, sharp_parts)
    branch, probe_vjp, logdet_terms, sharp_parts = lax.map(one_sequence, (inputs, probes, lengths))
    sharp_grad = lax.optimization_barrier(jnp.sum(sharp_parts, axis=0)) * (1.0 / (inputs.shape[0] * seq_total * head_size))
    w_wide = w_query.astype(jnp.float32)
    column = jnp.dot(start_vector, w_wide, precision=lax.Precision.HIGHEST)
    image_vec = jnp.dot(w_wide, column, precision=lax.Precision.HIGHEST)
    column_sq = jnp.sum(jnp.square(column))
    spec_vector = image_vec / jnp.sqrt(jnp.mean(jnp.square(image_vec)) + 1e-06)
    spec_norm = jnp.sqrt(jnp.sum(jnp.square(image_vec)) / (column_sq + 1e-06)).reshape(1)
    return (branch, probe_vjp, logdet_terms, sharp_grad, spec_vector, spec_norm)
```

```python
import functools
import math

import jax
import jax.numpy as jnp
from jax import lax
from jax.experimental import pallas as pl
from jax.experimental.pallas import tpu as pltpu
from jax.sharding import PartitionSpec as P

DH = 64
F32 = jnp.float32
BF16 = jnp.bfloat16


def dot(a, b, ca, cb):
    return lax.dot_general(a, b, (((ca,), (cb,)), ((), ())), preferred_element_type=F32)


def attention_kernel(heads, ndp, qc_ref, w_ref, sharp_ref, pat_ref, len_ref, start_ref, branch_ref,
                     vjp_ref, stat_ref, spec_ref, image, cols, own, other_part, box_a, box_g, home_a, home_g, left_rows,
                     grad_rows, adjoint_out, w_all, seq_tile, dp_tile, w_sem, a_send, a_recv, g_send,
                     g_recv, s_send, s_recv, d_send, d_recv):
    blocks, width, pair = qc_ref.shape
    span = pair // 2
    depth = w_all.shape[1]
    me, d = lax.axis_index("seq"), lax.axis_index("dp")
    length = len_ref[0]
    mesh_id = pl.DeviceIdType.MESH

    fetch = pltpu.make_async_copy(w_ref, w_all, w_sem)
    fetch.start()
    barrier = pltpu.get_barrier_semaphore()
    for k in range(1, blocks):
        pl.semaphore_signal(barrier, inc=1, device_id={"seq": (me + k) % blocks, "dp": d},
                            device_id_type=mesh_id)
    for k in range(1, ndp):
        pl.semaphore_signal(barrier, inc=1, device_id={"seq": me, "dp": (d + k) % ndp},
                            device_id_type=mesh_id)

    def push(src, dst, send, recv, target, t_dp):
        return pltpu.make_async_remote_copy(
            src_ref=src, dst_ref=dst, send_sem=send, recv_sem=recv,
            device_id={"seq": target, "dp": t_dp}, device_id_type=mesh_id)

    def push_a(i):
        return push(box_a.at[i], home_a.at[me], a_send.at[i], a_recv.at[me], i, d)

    def push_g(i):
        return push(box_g.at[i], home_g.at[me], g_send.at[i], g_recv.at[me], i, d)

    def push_s(i):
        return push(seq_tile.at[me], seq_tile.at[me], s_send.at[i], s_recv.at[me], i, d)

    def push_d(j):
        return push(dp_tile.at[d], dp_tile.at[d], d_send.at[j], d_recv.at[d], me, j)

    def arrived(ref, sem):
        pltpu.make_async_copy(ref, ref, sem).wait()

    def prepare(i, carry):
        q = qc_ref[i, :, :span].astype(F32)
        c = qc_ref[i, :, span:].astype(F32)
        rows = [jnp.sum((q * q)[h * DH:(h + 1) * DH], axis=0, keepdims=True) for h in range(heads)]
        rows += [jnp.sum((q * c)[h * DH:(h + 1) * DH], axis=0, keepdims=True) for h in range(heads)]
        if 2 * heads < 8:
            rows.append(jnp.zeros((8 - 2 * heads, span), F32))
        cols[i] = jnp.transpose(jnp.concatenate(rows, axis=0))
        return carry

    lax.fori_loop(0, blocks, prepare, 0)
    sharp_at = dp_tile.at[d]
    sharp_at[...] = jnp.zeros((8, span), F32)
    key_at = lax.broadcasted_iota(jnp.int32, (span, span), 0)
    query_at = lax.broadcasted_iota(jnp.int32, (span, span), 1)
    tail = (lax.broadcasted_iota(jnp.int32, (16, 2 * span), 1) < span).astype(F32).astype(BF16)
    pl.semaphore_wait(barrier, blocks + ndp - 2)

    def block(k, carry):
        i = (me + blocks // 2 + k) % blocks
        other = pat_ref[1, i]
        allowed = jnp.concatenate(
            [(i * span + key_at < length) | (key_at == query_at), other * span + key_at < length],
            axis=0)
        for h in range(heads):
            hs = slice(h * DH, (h + 1) * DH)
            qc = qc_ref[i, hs, :]
            qc_other = qc_ref[other, hs, :]
            q = qc[:, :span]
            c = qc[:, span:]
            keys = jnp.concatenate([q, qc_other[:, :span]], axis=1)
            key_cots = jnp.concatenate([c, qc_other[:, span:]], axis=1)
            both = dot(keys, qc, 0, 0)
            inner = both[:, :span]
            prob_grad = both[:, span:]
            cross = dot(key_cots, q, 0, 0)
            qf = q.astype(F32)
            cf = c.astype(F32)
            norm_row = jnp.sum(qf * qf, axis=0, keepdims=True)
            pair_row = jnp.sum(qf * cf, axis=0, keepdims=True)
            norm_col = jnp.concatenate([cols[i, :, h:h + 1], cols[other, :, h:h + 1]], axis=0)
            pair_col = jnp.concatenate(
                [cols[i, :, heads + h:heads + h + 1], cols[other, :, heads + h:heads + h + 1]], axis=0)
            factor = sharp_ref[h] * (1.0 / math.sqrt(DH))
            distance = norm_row + norm_col - 2.0 * inner
            weights = jnp.where(allowed, jnp.exp(-factor * distance), 0.0)
            total = jnp.sum(weights, axis=0, keepdims=True)
            soft = weights * (1.0 / total)
            low = soft.astype(BF16)
            row_inner = jnp.sum(soft * prob_grad, axis=0, keepdims=True)
            score = soft * (prob_grad - row_inner)
            dp_tile[d, h:h + 1, :] += jnp.sum(score * distance, axis=0, keepdims=True)
            coef = (-2.0 * factor * score).astype(BF16)
            row_total = jnp.sum(coef.astype(F32), axis=0, keepdims=True)
            gap = pair_row + pair_col - cross - prob_grad
            gap_mean = jnp.sum(soft * gap, axis=0, keepdims=True)
            adj = (-2.0 * factor * (soft * (gap - gap_mean))).astype(BF16)
            mixed = jnp.concatenate([coef, low], axis=1)
            left = dot(keys, mixed, 1, 0)
            box_a[i, 0, hs, :] = left[:, span:].astype(BF16)
            adjoint = dot(jnp.concatenate([keys, key_cots], axis=1),
                          jnp.concatenate([adj, low], axis=0), 1, 0)
            box_a[i, 1, hs, :] = adjoint.astype(BF16)
            lhs = jnp.concatenate([jnp.concatenate([-q, c], axis=1), tail], axis=0)
            right = dot(lhs, mixed, 1, 1)
            key_part = keys.astype(F32) * right[DH:DH + 1, :] + right[:DH]
            own[i, hs, :] = qf * row_total - left[:, :span] + key_part[:, :span]
            other_part[i, hs, :] = key_part[:, span:]
        pl.when(i != me)(lambda: push_a(i).start())
        return carry

    lax.fori_loop(0, blocks, block, 0)

    def finish(k, term):
        m = (me + blocks // 2 + k) % blocks

        def gather(i, total):
            chosen = jnp.where(pat_ref[1, i] == m, 1.0, 0.0)
            return total + other_part[i] * chosen

        if blocks <= 8:
            g = own[m]
            for i in range(blocks):
                g = gather(i, g)
        else:
            g = lax.fori_loop(0, blocks, gather, own[m])
        box_g[m] = g.astype(BF16)
        pl.when(m != me)(lambda: push_g(m).start())
        return term + jnp.sum(g * qc_ref[m, :, span:].astype(F32), axis=0, keepdims=True)

    term_one = lax.fori_loop(0, blocks, finish, jnp.zeros((1, span), F32))
    for k in range(1, ndp):
        push_d((d + k) % ndp).start()
    home_a[me] = box_a[me]
    home_g[me] = box_g[me]
    fetch.wait()

    def take_a(k, carry):
        s = (me + k) % blocks
        pl.when(k > 0)(lambda: arrived(home_a.at[s], a_recv.at[s]))
        left_rows[s, :2 * span, :] = jnp.concatenate(
            [jnp.transpose(home_a[s, 0]), jnp.transpose(home_a[s, 1])], axis=0)
        return carry

    def split(v):
        high = v.astype(BF16).astype(F32)
        mid = (v - high).astype(BF16).astype(F32)
        rows = [high, mid, v - high - mid, jnp.zeros((13, v.shape[1]), F32)]
        return jnp.concatenate(rows, axis=0).astype(BF16)

    start_rows = split(start_ref[...])

    def power(s, total):
        column = jnp.sum(dot(start_rows, w_all[s], 1, 0), axis=0, keepdims=True)
        left_rows[s, 2 * span:, :] = split(column)
        return total + column * column

    column_sq = lax.fori_loop(0, blocks, power, jnp.zeros((1, width), F32))
    lax.fori_loop(0, blocks, take_a, 0)
    step = 256

    def product(rows_ref, r):
        at = pl.ds(pl.multiple_of(r * step, step), step)
        total = jnp.zeros((rows_ref.shape[1], step), F32)
        for s in range(blocks):
            total = total + dot(rows_ref[s], w_all[s, at, :], 1, 1)
        return at, total

    def outward(r, carry):
        at, total = product(left_rows, r)
        branch_ref[:, at] = total[:span].astype(BF16)
        adjoint_out[:, at] = total[span:2 * span]
        image[:, at] = jnp.sum(total[2 * span:], axis=0, keepdims=True)
        return carry

    lax.fori_loop(0, depth // step, outward, 0)

    def take_g(k, carry):
        s = (me + k) % blocks
        pl.when(k > 0)(lambda: arrived(home_g.at[s], g_recv.at[s]))
        grad_rows[s] = jnp.transpose(home_g[s])
        return carry

    lax.fori_loop(0, blocks, take_g, 0)

    def backward(r, term):
        at, total = product(grad_rows, r)
        low = total.astype(BF16)
        vjp_ref[:, at] = low
        part = low.astype(F32) * adjoint_out[:, at]
        for n in range(step // span):
            term = term + jnp.sum(part[:, n * span:(n + 1) * span], axis=0, keepdims=True)
        return term

    image_sq = jnp.sum(image[...] * image[...], axis=1, keepdims=True)
    spec_ref[...] = image[...] / jnp.sqrt(image_sq / depth + 1e-06)
    norm = jnp.sqrt(image_sq / (jnp.sum(column_sq, axis=1, keepdims=True) + 1e-06))
    stat_ref[16:] = jnp.broadcast_to(norm, (8, span))
    term_two = lax.fori_loop(0, depth // step, backward, jnp.zeros((1, span), F32))
    seq_tile[me] = jnp.concatenate([term_one, term_two, jnp.zeros((6, span), F32)], axis=0)
    for k in range(1, blocks):
        push_s((me + k) % blocks).start()
    for k in range(1, ndp):
        j = (d + k) % ndp
        arrived(dp_tile.at[j], d_recv.at[j])
        push_d(j).wait_send()
    for k in range(1, blocks):
        i = (me + k) % blocks
        push_a(i).wait_send()
        push_g(i).wait_send()
        arrived(seq_tile.at[i], s_recv.at[i])
        push_s(i).wait_send()
    stat_ref[:8] = jnp.broadcast_to(
        jnp.sum(jnp.sum(seq_tile[...], axis=0), axis=1, keepdims=True), (8, span))
    stat_ref[8:16] = jnp.broadcast_to(
        jnp.sum(jnp.sum(dp_tile[...], axis=0), axis=1, keepdims=True), (8, span))


def attention(ndp, qc, w_all, sharpness, pattern, lengths, start_vector):
    blocks, width, pair = qc.shape
    span = pair // 2
    depth = w_all.shape[1]
    heads = sharpness.shape[0]
    smem = pl.BlockSpec(memory_space=pltpu.SMEM)
    vmem = pl.BlockSpec(memory_space=pltpu.VMEM)
    sem = pltpu.SemaphoreType.DMA
    return pl.pallas_call(
        functools.partial(attention_kernel, heads, ndp),
        out_shape=(jax.ShapeDtypeStruct((span, depth), BF16),
                   jax.ShapeDtypeStruct((span, depth), BF16),
                   jax.ShapeDtypeStruct((24, span), F32),
                   jax.ShapeDtypeStruct((1, depth), F32)),
        in_specs=[vmem, pl.BlockSpec(memory_space=pl.ANY), smem, smem, smem, vmem],
        out_specs=(vmem, vmem, vmem, vmem),
        scratch_shapes=[pltpu.VMEM((1, depth), F32),
                        pltpu.VMEM((blocks, span, max(8, 2 * heads)), F32),
                        pltpu.VMEM((blocks, width, span), F32),
                        pltpu.VMEM((blocks, width, span), F32),
                        pltpu.VMEM((blocks, 2, width, span), BF16),
                        pltpu.VMEM((blocks, width, span), BF16),
                        pltpu.VMEM((blocks, 2, width, span), BF16),
                        pltpu.VMEM((blocks, width, span), BF16),
                        pltpu.VMEM((blocks, 2 * span + 16, width), BF16),
                        pltpu.VMEM((blocks, span, width), BF16),
                        pltpu.VMEM((span, depth), F32),
                        pltpu.VMEM((blocks, depth, width), BF16),
                        pltpu.VMEM((blocks, 8, span), F32),
                        pltpu.VMEM((ndp, 8, span), F32),
                        sem, sem((blocks,)), sem((blocks,)), sem((blocks,)), sem((blocks,)),
                        sem((blocks,)), sem((blocks,)), sem((ndp,)), sem((ndp,))],
        compiler_params=pltpu.CompilerParams(collective_id=1, has_side_effects=True,
                                             vmem_limit_bytes=56 * 1024 * 1024),
        name="attention",
    )(qc, w_all, sharpness, pattern, lengths, start_vector.reshape(1, depth))


def keep_kernel(scale_term, scale_sharp, a_ref, b_ref, stat_ref, spec_ref, len_ref, a_out, b_out, term_out,
                sharp_out, spec_out, norm_out):
    a_out[...] = a_ref[...]
    b_out[...] = b_ref[...]
    spec_out[...] = spec_ref[...]
    span = stat_ref.shape[1]
    row_at = lax.broadcasted_iota(jnp.int32, (8, span), 0)
    column_at = lax.broadcasted_iota(jnp.int32, (8, span), 1)

    def as_row(at):
        return jnp.sum(jnp.where(row_at == column_at, stat_ref[at:at + 8], 0.0), axis=0, keepdims=True)

    count = jnp.full((1, span), len_ref[0], jnp.int32).astype(F32) * scale_term
    term_out[...] = (as_row(0) / count)[:, :term_out.shape[1]]
    sharp_out[...] = (as_row(8) * scale_sharp)[:, :sharp_out.shape[1]]
    norm_out[...] = stat_ref[16:17, :1]


def keep(a, b, stats, spec, lengths, heads, scale_term, scale_sharp):
    smem = pl.BlockSpec(memory_space=pltpu.SMEM)
    vmem = pl.BlockSpec(memory_space=pltpu.VMEM)
    return pl.pallas_call(
        functools.partial(keep_kernel, scale_term, scale_sharp),
        out_shape=(jax.ShapeDtypeStruct(a.shape, a.dtype), jax.ShapeDtypeStruct(b.shape, b.dtype),
                   jax.ShapeDtypeStruct((1, 2), F32), jax.ShapeDtypeStruct((1, heads), F32),
                   jax.ShapeDtypeStruct(spec.shape, F32), jax.ShapeDtypeStruct((1, 1), F32)),
        in_specs=[vmem, vmem, vmem, vmem, smem],
        out_specs=(vmem,) * 6, name="keep")(a, b, stats, spec, lengths)


def gather_kernel(ndp, groups, x_ref, p_ref, w_ref, len_ref, w_out, got, both, outbox, recv, send, a2a_recv, a2a_send):
    span, depth = x_ref.shape
    width = w_ref.shape[1]
    lines, rows = groups // 2, depth // ndp
    ys = ndp // 2
    me, d = lax.axis_index("seq"), lax.axis_index("dp")
    z, x = me // 2, me % 2
    y, core = d // 2, d % 2

    def seq_id(s):
        return {"seq": s, "dp": d}

    def dp_id(t):
        return {"seq": me, "dp": t}

    barrier = pltpu.get_barrier_semaphore()
    for k in range(1, groups):
        pl.semaphore_signal(barrier, inc=1, device_id=seq_id((me + k) % groups),
                            device_id_type=pl.DeviceIdType.MESH)
    pl.semaphore_signal(barrier, inc=1, device_id=dp_id(d + 1 - 2 * core),
                        device_id_type=pl.DeviceIdType.MESH)
    for k in range(1, ys):
        pl.semaphore_signal(barrier, inc=1, device_id=dp_id(((y + k) % ys) * 2 + core),
                            device_id_type=pl.DeviceIdType.MESH)
    pl.semaphore_wait(barrier, groups + ys - 1)

    def piece(s, owner, kind, target, own=False):
        at = pl.ds(pl.multiple_of(owner * rows, rows), rows)
        src = w_ref.at[at] if own else w_out.at[s, at]
        return pltpu.make_async_remote_copy(
            src_ref=src, dst_ref=w_out.at[s, at], send_sem=send.at[kind, s],
            recv_sem=recv.at[owner, s], device_id=target, device_id_type=pl.DeviceIdType.MESH)

    def landed(s, owner):
        at = pl.ds(pl.multiple_of(owner * rows, rows), rows)
        pltpu.make_async_copy(w_out.at[s, at], w_out.at[s, at], recv.at[owner, s]).wait()

    up, down, across = seq_id((me + 2) % groups), seq_id((me + groups - 2) % groups), seq_id(me + 1 - 2 * x)
    mate = dp_id(d + 1 - 2 * core)

    def order(t):
        p, side = t // 2, t % 2
        m = jnp.minimum(z, lines - 1 - z)
        near = jnp.where(p % 2 == 1, z + (p + 1) // 2, z - p // 2)
        far = jnp.where(2 * z < lines, p, lines - 1 - p)
        zs = jnp.where(p <= 2 * m, near, far)
        xs = (x + side) % 2
        return zs * 2 + xs, zs, xs

    pl.when(z + 1 < lines)(lambda: piece(me, d, 0, up, True).start())
    pl.when(z > 0)(lambda: piece(me, d, 1, down, True).start())
    piece(me, d, 2, across, True).start()
    for k in range(1, ys):
        piece(me, ((y + k) % ys) * 2 + core, 3 + k, across, True).start()
    w_out[me] = w_ref[...]
    both[:span] = x_ref[...]
    valid = me * span + lax.broadcasted_iota(jnp.int32, (span, 1), 0) < len_ref[0]
    both[span:] = jnp.where(valid, p_ref[...].astype(F32), 0.0).astype(BF16)

    def stage_a(t):
        s, zs, xs = order(t)
        landed(s, d)

        @pl.when(xs == x)
        def _():
            pl.when((zs < z) & (z + 1 < lines))(lambda: piece(s, d, 0, up).start())
            pl.when((zs > z) & (z > 0))(lambda: piece(s, d, 1, down).start())
            piece(s, d, 2, across).start()

        @pl.when(t > 1)
        def _():
            for k in range(1, ys):
                piece(s, d, 3 + k, dp_id(((y + k) % ys) * 2 + core)).start()

        piece(s, d, 3, mate).start()

    def stage_b(t):
        s, zs, xs = order(t)
        for k in range(1, ys):
            owner = ((y + k) % ys) * 2 + core
            landed(s, owner)
            piece(s, owner, 2 + ys + k, mate).start()

    def out_copy(s):
        return pltpu.make_async_remote_copy(
            src_ref=outbox.at[s], dst_ref=got.at[me], send_sem=a2a_send.at[s],
            recv_sem=a2a_recv.at[me], device_id=seq_id(s), device_id_type=pl.DeviceIdType.MESH)

    def stage_c(t):
        s, zs, xs = order(t)

        @pl.when(t > 0)
        def _():
            for k in range(ys):
                landed(s, ((y + k) % ys) * 2 + 1 - core)

        w = w_out[s]
        res = jnp.transpose(dot(both[...], w, 1, 0)).astype(BF16)

        @pl.when(t > 0)
        def _():
            outbox[s] = res
            out_copy(s).start()

        @pl.when(t == 0)
        def _():
            got[me] = res

    lag_b, lag_c = 2, 3

    def tick(t, carry):
        pl.when((t > 0) & (t < groups))(lambda: stage_a(t))
        pl.when((t - lag_b > 0) & (t - lag_b < groups))(lambda: stage_b(t - lag_b))
        pl.when(t - lag_c >= 0)(lambda: stage_c(t - lag_c))
        return carry

    lax.fori_loop(0, groups + lag_c, tick, 0)

    def drain(t, carry):
        s, zs, xs = order(t)
        pl.when((xs == x) & (zs <= z) & (z + 1 < lines))(lambda: piece(s, d, 0, up).wait_send())
        pl.when((xs == x) & (zs >= z) & (z > 0))(lambda: piece(s, d, 1, down).wait_send())
        pl.when(xs == x)(lambda: piece(s, d, 2, across).wait_send())

        @pl.when(t != 1)
        def _():
            for k in range(1, ys):
                piece(s, d, 3 + k, mate).wait_send()

        @pl.when(t > 0)
        def _():
            for k in range(1, ys):
                piece(s, d, 2 + ys + k, mate).wait_send()
            piece(s, d, 3, mate).wait_send()
            out_copy(s).wait_send()
            pltpu.make_async_copy(got.at[s], got.at[s], a2a_recv.at[s]).wait()

        return carry

    lax.fori_loop(0, groups, drain, 0)


def gather_project(ndp, groups, tokens, probe_rows, w_query, lengths):
    span, depth = tokens.shape
    width = w_query.shape[1]
    smem = pl.BlockSpec(memory_space=pltpu.SMEM)
    vmem = pl.BlockSpec(memory_space=pltpu.VMEM)
    return pl.pallas_call(
        functools.partial(gather_kernel, ndp, groups),
        out_shape=(jax.ShapeDtypeStruct((groups, depth, width), BF16),
                   jax.ShapeDtypeStruct((groups, width, 2 * span), BF16)),
        in_specs=[vmem, vmem, vmem, smem],
        out_specs=(vmem, vmem),
        scratch_shapes=[pltpu.VMEM((2 * span, depth), BF16),
                        pltpu.VMEM((groups, width, 2 * span), BF16),
                        pltpu.SemaphoreType.DMA((ndp, groups)),
                        pltpu.SemaphoreType.DMA((2 + ndp, groups)),
                        pltpu.SemaphoreType.DMA((groups,)),
                        pltpu.SemaphoreType.DMA((groups,))],
        compiler_params=pltpu.CompilerParams(collective_id=0, has_side_effects=True,
                                             vmem_limit_bytes=56 * 1024 * 1024),
        name="gather_project",
    )(tokens, probe_rows, w_query, lengths)


def shards(inputs, w_query, sharpness, pattern, lengths, probes, start_vector):
    tokens = inputs[0]
    probe_rows = probes[0]
    rows_here = tokens.shape[0]
    groups = lax.axis_size("seq")
    inner_here = w_query.shape[1]
    inner = inner_here * groups
    w_all, got = gather_project(
        lax.axis_size("dp"), groups, tokens, probe_rows, w_query, lengths)
    branch, probe_vjp, stats, spec = attention(
        lax.axis_size("dp"), got, w_all, sharpness, pattern.T, lengths, start_vector)
    heads = sharpness.shape[0]
    scale_sharp = -1.0 / math.sqrt(DH) / (lax.axis_size("dp") * groups * rows_here * DH)
    branch, probe_vjp, terms, sharp_grad, spec, norm = keep(
        branch, probe_vjp, stats, spec, lengths, heads, float(inner), scale_sharp)
    return (branch[None], probe_vjp[None], terms, sharp_grad.reshape(-1), spec.reshape(-1), norm.reshape(-1))


def solution(mesh):
    placed = (
        P("dp", "seq", None),
        P(None, "seq"),
        P("seq"),
        P(),
        P("dp"),
        P("dp", "seq", None),
        P(),
    )
    return jax.shard_map(
        shards,
        mesh=mesh,
        in_specs=placed,
        out_specs=(P("dp", "seq", None), P("dp", "seq", None), P("dp", None), P("seq"), P(), P()),
        check_vma=False,
    )
```

```python
import functools
import math

import jax
import jax.numpy as jnp
from jax import lax
from jax.experimental import pallas as pl
from jax.experimental.pallas import tpu as pltpu
from jax.sharding import PartitionSpec as P

DH = 64
F32 = jnp.float32
BF16 = jnp.bfloat16


def dot(a, b, ca, cb):
    return lax.dot_general(a, b, (((ca,), (cb,)), ((), ())), preferred_element_type=F32)


def layer_kernel(heads, ndp, x_ref, p_ref, w_ref, sharp_ref, pat_ref, len_ref, start_ref, branch_ref,
                 vjp_ref, stat_ref, spec_ref, both, outbox, qc_ref, image, cols, own, other_part, box_a, box_g,
                 home_a, home_g, left_rows, grad_rows, adjoint_out, w_all, seq_tile, dp_tile, loc_sem, x_send,
                 x_recv, w_send, w_recv, q_send, q_recv, a_send, a_recv, g_send, g_recv, s_send, s_recv, d_send,
                 d_recv):
    blocks, width, pair = qc_ref.shape
    span = pair // 2
    depth = w_all.shape[1]
    lines, ys, rows = blocks // 2, ndp // 2, depth // ndp
    me, d = lax.axis_index("seq"), lax.axis_index("dp")
    z, x = me // 2, me % 2
    y, core = d // 2, d % 2
    mate_d = d + 1 - 2 * core
    beside = me + 1 - 2 * x
    length = len_ref[0]
    mesh_id = pl.DeviceIdType.MESH

    loads = [pltpu.make_async_copy(w_ref, w_all.at[me], loc_sem.at[0]),
             pltpu.make_async_copy(x_ref, both.at[x, :span], loc_sem.at[1]),
             pltpu.make_async_copy(p_ref, both.at[x, span:], loc_sem.at[2])]
    for load in loads:
        load.start()
    barrier = pltpu.get_barrier_semaphore()
    for k in range(1, blocks):
        pl.semaphore_signal(barrier, inc=1, device_id={"seq": (me + k) % blocks, "dp": d},
                            device_id_type=mesh_id)
    for k in range(1, ndp):
        pl.semaphore_signal(barrier, inc=1, device_id={"seq": me, "dp": (d + k) % ndp},
                            device_id_type=mesh_id)
    pl.semaphore_wait(barrier, blocks + ndp - 2)

    def push(src, dst, send, recv, target, t_dp):
        return pltpu.make_async_remote_copy(
            src_ref=src, dst_ref=dst, send_sem=send, recv_sem=recv,
            device_id={"seq": target, "dp": t_dp}, device_id_type=mesh_id)

    def push_a(i):
        return push(box_a.at[i], home_a.at[me], a_send.at[i], a_recv.at[me], i, d)

    def push_g(i):
        return push(box_g.at[i], home_g.at[me], g_send.at[i], g_recv.at[me], i, d)

    def push_s(i):
        return push(seq_tile.at[me], seq_tile.at[me], s_send.at[i], s_recv.at[me], i, d)

    def push_d(j):
        return push(dp_tile.at[d], dp_tile.at[d], d_send.at[j], d_recv.at[d], me, j)

    def arrived(ref, sem):
        pltpu.make_async_copy(ref, ref, sem).wait()

    def push_x():
        return push(x_ref, both.at[x, :span], x_send.at[0], x_recv.at[0], beside, d)

    def push_p():
        return push(p_ref, both.at[x, span:], x_send.at[1], x_recv.at[1], beside, d)

    def part(owner):
        return pl.ds(pl.multiple_of(owner * rows, rows), rows)

    def piece(s, owner, kind, target, t_dp, first=False):
        src = w_ref.at[part(owner)] if first else w_all.at[s, part(owner)]
        return push(src, w_all.at[s, part(owner)], w_send.at[kind, s], w_recv.at[owner, s], target, t_dp)

    def landed(s, owner):
        arrived(w_all.at[s, part(owner)], w_recv.at[owner, s])

    up, down = (me + 2) % blocks, (me + blocks - 2) % blocks

    def line(t):
        m = jnp.minimum(z, lines - 1 - z)
        near = jnp.where(t % 2 == 1, z + (t + 1) // 2, z - t // 2)
        far = jnp.where(2 * z < lines, t, lines - 1 - t)
        return jnp.where(t <= 2 * m, near, far)

    def spread(s):
        landed(s, d)
        for k in range(1, ys):
            piece(s, d, 3 + k, me, ((y + k) % ys) * 2 + core).start()
        piece(s, d, 3, me, mate_d).start()

    def relay(s):
        for k in range(1, ys):
            owner = ((y + k) % ys) * 2 + core
            landed(s, owner)
            piece(s, owner, 2 + ys + k, me, mate_d).start()

    def complete(s):
        for k in range(ys):
            landed(s, ((y + k) % ys) * 2 + 1 - core)

    def spread_done(s):
        for k in range(1, ys):
            piece(s, d, 3 + k, me, d).wait_send()
            piece(s, d, 2 + ys + k, me, d).wait_send()
        piece(s, d, 3, me, d).wait_send()

    pl.when(z + 1 < lines)(lambda: piece(me, d, 0, up, d, True).start())
    pl.when(z > 0)(lambda: piece(me, d, 1, down, d, True).start())
    push_x().start()
    push_p().start()
    query_row = lax.broadcasted_iota(jnp.int32, (1, pair), 1)

    def project(s, side):
        res = jnp.transpose(dot(both[side], w_all[s], 1, 0))
        kept = (query_row < span) | ((z * 2 + side) * span + query_row - span < length)
        return jnp.where(kept, res, 0.0).astype(BF16)

    def push_q(line_at, side):
        return push(outbox.at[line_at, side], qc_ref.at[z * 2 + side], q_send.at[line_at, side],
                    q_recv.at[z * 2 + side], line_at * 2 + x, d)

    for load in loads:
        load.wait()
    qc_ref[me] = project(me, x)

    def tick(t, carry):
        @pl.when(t < lines)
        def _():
            at = line(t)
            s = at * 2 + x
            landed_first(s, at)

        @pl.when((t > 1) & (t - 1 < lines))
        def _():
            relay(line(t - 1) * 2 + x)

        @pl.when(t > 2)
        def _():
            at = line(t - 2)
            complete(at * 2 + x)
            outbox[at, x] = project(at * 2 + x, x)
            push_q(at, x).start()

        return carry

    def landed_first(s, at):
        landed(s, d)
        pl.when((at < z) & (z + 1 < lines))(lambda: piece(s, d, 0, up, d).start())
        pl.when((at > z) & (z > 0))(lambda: piece(s, d, 1, down, d).start())
        for k in range(1, ys):
            piece(s, d, 3 + k, me, ((y + k) % ys) * 2 + core).start()
        piece(s, d, 3, me, mate_d).start()

    lax.fori_loop(1, lines + 2, tick, 0)
    arrived(both.at[1 - x, :span], x_recv.at[0])
    arrived(both.at[1 - x, span:], x_recv.at[1])

    def partner(t, carry):
        at = line(t)
        outbox[at, 1 - x] = project(at * 2 + x, 1 - x)
        push_q(at, 1 - x).start()
        return carry

    lax.fori_loop(1, lines, partner, 0)

    def across(t, carry):
        piece(line(t) * 2 + x, d, 2, beside, d).start()
        return carry

    lax.fori_loop(0, lines, across, 0)
    qc_ref[beside] = project(me, 1 - x)

    def prepare(k, carry):
        i = (me - x + k) % blocks
        pl.when(k > 1)(lambda: arrived(qc_ref.at[i], q_recv.at[i]))
        q = qc_ref[i, :, :span].astype(F32)
        c = qc_ref[i, :, span:].astype(F32)
        rows = [jnp.sum((q * q)[h * DH:(h + 1) * DH], axis=0, keepdims=True) for h in range(heads)]
        rows += [jnp.sum((q * c)[h * DH:(h + 1) * DH], axis=0, keepdims=True) for h in range(heads)]
        if 2 * heads < 8:
            rows.append(jnp.zeros((8 - 2 * heads, span), F32))
        cols[i] = jnp.transpose(jnp.concatenate(rows, axis=0))
        return carry

    lax.fori_loop(0, blocks, prepare, 0)
    sharp_at = dp_tile.at[d]
    sharp_at[...] = jnp.zeros((8, span), F32)
    key_at = lax.broadcasted_iota(jnp.int32, (span, span), 0)
    query_at = lax.broadcasted_iota(jnp.int32, (span, span), 1)
    tail = (lax.broadcasted_iota(jnp.int32, (16, 2 * span), 1) < span).astype(F32).astype(BF16)

    def block(k, carry):
        i = (me + blocks // 2 + k) % blocks
        other = pat_ref[1, i]
        allowed = jnp.concatenate(
            [(i * span + key_at < length) | (key_at == query_at), other * span + key_at < length],
            axis=0)
        for h in range(heads):
            hs = slice(h * DH, (h + 1) * DH)
            qc = qc_ref[i, hs, :]
            qc_other = qc_ref[other, hs, :]
            q = qc[:, :span]
            c = qc[:, span:]
            keys = jnp.concatenate([q, qc_other[:, :span]], axis=1)
            key_cots = jnp.concatenate([c, qc_other[:, span:]], axis=1)
            both = dot(keys, qc, 0, 0)
            inner = both[:, :span]
            prob_grad = both[:, span:]
            cross = dot(key_cots, q, 0, 0)
            qf = q.astype(F32)
            cf = c.astype(F32)
            norm_row = jnp.sum(qf * qf, axis=0, keepdims=True)
            pair_row = jnp.sum(qf * cf, axis=0, keepdims=True)
            norm_col = jnp.concatenate([cols[i, :, h:h + 1], cols[other, :, h:h + 1]], axis=0)
            pair_col = jnp.concatenate(
                [cols[i, :, heads + h:heads + h + 1], cols[other, :, heads + h:heads + h + 1]], axis=0)
            factor = sharp_ref[h] * (1.0 / math.sqrt(DH))
            distance = norm_row + norm_col - 2.0 * inner
            weights = jnp.where(allowed, jnp.exp(-factor * distance), 0.0)
            total = jnp.sum(weights, axis=0, keepdims=True)
            soft = weights * (1.0 / total)
            low = soft.astype(BF16)
            row_inner = jnp.sum(soft * prob_grad, axis=0, keepdims=True)
            score = soft * (prob_grad - row_inner)
            dp_tile[d, h:h + 1, :] += jnp.sum(score * distance, axis=0, keepdims=True)
            coef = (-2.0 * factor * score).astype(BF16)
            row_total = jnp.sum(coef.astype(F32), axis=0, keepdims=True)
            gap = pair_row + pair_col - cross - prob_grad
            gap_mean = jnp.sum(soft * gap, axis=0, keepdims=True)
            adj = (-2.0 * factor * (soft * (gap - gap_mean))).astype(BF16)
            mixed = jnp.concatenate([coef, low], axis=1)
            left = dot(keys, mixed, 1, 0)
            box_a[i, 0, hs, :] = left[:, span:].astype(BF16)
            adjoint = dot(jnp.concatenate([keys, key_cots], axis=1),
                          jnp.concatenate([adj, low], axis=0), 1, 0)
            box_a[i, 1, hs, :] = adjoint.astype(BF16)
            lhs = jnp.concatenate([jnp.concatenate([-q, c], axis=1), tail], axis=0)
            right = dot(lhs, mixed, 1, 1)
            key_part = keys.astype(F32) * right[DH:DH + 1, :] + right[:DH]
            own[i, hs, :] = qf * row_total - left[:, :span] + key_part[:, :span]
            other_part[i, hs, :] = key_part[:, span:]
        pl.when(i != me)(lambda: push_a(i).start())
        pl.when(k < lines)(lambda: spread(line(k) * 2 + 1 - x))
        pl.when((k > 1) & (k - 2 < lines))(lambda: relay(line(k - 2) * 2 + 1 - x))
        return carry

    lax.fori_loop(0, blocks, block, 0)

    def finish(k, term):
        m = (me + blocks // 2 + k) % blocks

        def gather(i, total):
            chosen = jnp.where(pat_ref[1, i] == m, 1.0, 0.0)
            return total + other_part[i] * chosen

        if blocks <= 8:
            g = own[m]
            for i in range(blocks):
                g = gather(i, g)
        else:
            g = lax.fori_loop(0, blocks, gather, own[m])
        box_g[m] = g.astype(BF16)
        pl.when(m != me)(lambda: push_g(m).start())
        return term + jnp.sum(g * qc_ref[m, :, span:].astype(F32), axis=0, keepdims=True)

    term_one = lax.fori_loop(0, blocks, finish, jnp.zeros((1, span), F32))
    for k in range(1, ndp):
        push_d((d + k) % ndp).start()
    home_a[me] = box_a[me]
    home_g[me] = box_g[me]

    def whole(t, carry):
        complete(line(t) * 2 + 1 - x)
        return carry

    lax.fori_loop(0, lines, whole, 0)

    def take_a(k, carry):
        s = (me + k) % blocks
        pl.when(k > 0)(lambda: arrived(home_a.at[s], a_recv.at[s]))
        left_rows[s, :2 * span, :] = jnp.concatenate(
            [jnp.transpose(home_a[s, 0]), jnp.transpose(home_a[s, 1])], axis=0)
        return carry

    def split(v):
        high = v.astype(BF16).astype(F32)
        mid = (v - high).astype(BF16).astype(F32)
        rows = [high, mid, v - high - mid, jnp.zeros((13, v.shape[1]), F32)]
        return jnp.concatenate(rows, axis=0).astype(BF16)

    start_rows = split(start_ref[...])

    def power(s, total):
        column = jnp.sum(dot(start_rows, w_all[s], 1, 0), axis=0, keepdims=True)
        left_rows[s, 2 * span:, :] = split(column)
        return total + column * column

    column_sq = lax.fori_loop(0, blocks, power, jnp.zeros((1, width), F32))
    lax.fori_loop(0, blocks, take_a, 0)
    step = 256

    def product(rows_ref, r):
        at = pl.ds(pl.multiple_of(r * step, step), step)
        total = jnp.zeros((rows_ref.shape[1], step), F32)
        for s in range(blocks):
            total = total + dot(rows_ref[s], w_all[s, at, :], 1, 1)
        return at, total

    def outward(r, carry):
        at, total = product(left_rows, r)
        branch_ref[:, at] = total[:span].astype(BF16)
        adjoint_out[:, at] = total[span:2 * span]
        image[:, at] = jnp.sum(total[2 * span:], axis=0, keepdims=True)
        return carry

    lax.fori_loop(0, depth // step, outward, 0)

    def take_g(k, carry):
        s = (me + k) % blocks
        pl.when(k > 0)(lambda: arrived(home_g.at[s], g_recv.at[s]))
        grad_rows[s] = jnp.transpose(home_g[s])
        return carry

    lax.fori_loop(0, blocks, take_g, 0)

    def backward(r, term):
        at, total = product(grad_rows, r)
        low = total.astype(BF16)
        vjp_ref[:, at] = low
        part = low.astype(F32) * adjoint_out[:, at]
        for n in range(step // span):
            term = term + jnp.sum(part[:, n * span:(n + 1) * span], axis=0, keepdims=True)
        return term

    image_sq = jnp.sum(image[...] * image[...], axis=1, keepdims=True)
    spec_ref[...] = image[...] / jnp.sqrt(image_sq / depth + 1e-06)
    norm = jnp.sqrt(image_sq / (jnp.sum(column_sq, axis=1, keepdims=True) + 1e-06))
    stat_ref[16:] = jnp.broadcast_to(norm, (8, span))
    term_two = lax.fori_loop(0, depth // step, backward, jnp.zeros((1, span), F32))
    seq_tile[me] = jnp.concatenate([term_one, term_two, jnp.zeros((6, span), F32)], axis=0)
    for k in range(1, blocks):
        push_s((me + k) % blocks).start()
    for k in range(1, ndp):
        j = (d + k) % ndp
        arrived(dp_tile.at[j], d_recv.at[j])
        push_d(j).wait_send()
    for k in range(1, blocks):
        i = (me + k) % blocks
        push_a(i).wait_send()
        push_g(i).wait_send()
        arrived(seq_tile.at[i], s_recv.at[i])
        push_s(i).wait_send()
    push_x().wait_send()
    push_p().wait_send()

    def drain(t, carry):
        at = line(t)
        s = at * 2 + x
        pl.when((at <= z) & (z + 1 < lines))(lambda: piece(s, d, 0, up, d).wait_send())
        pl.when((at >= z) & (z > 0))(lambda: piece(s, d, 1, down, d).wait_send())
        piece(s, d, 2, beside, d).wait_send()
        spread_done(at * 2 + 1 - x)

        @pl.when(t > 0)
        def _():
            spread_done(s)
            push_q(at, 0).wait_send()
            push_q(at, 1).wait_send()

        return carry

    lax.fori_loop(0, lines, drain, 0)
    stat_ref[:8] = jnp.broadcast_to(
        jnp.sum(jnp.sum(seq_tile[...], axis=0), axis=1, keepdims=True), (8, span))
    stat_ref[8:16] = jnp.broadcast_to(
        jnp.sum(jnp.sum(dp_tile[...], axis=0), axis=1, keepdims=True), (8, span))


def layer(ndp, groups, tokens, probe_rows, w_query, sharpness, pattern, lengths, start_vector):
    span, depth = tokens.shape
    width = w_query.shape[1]
    blocks, lines = groups, groups // 2
    heads = sharpness.shape[0]
    smem = pl.BlockSpec(memory_space=pltpu.SMEM)
    vmem = pl.BlockSpec(memory_space=pltpu.VMEM)
    hbm = pl.BlockSpec(memory_space=pl.ANY)
    sem = pltpu.SemaphoreType.DMA
    return pl.pallas_call(
        functools.partial(layer_kernel, heads, ndp),
        out_shape=(jax.ShapeDtypeStruct((span, depth), BF16),
                   jax.ShapeDtypeStruct((span, depth), BF16),
                   jax.ShapeDtypeStruct((24, span), F32),
                   jax.ShapeDtypeStruct((1, depth), F32)),
        in_specs=[hbm, hbm, hbm, smem, smem, smem, vmem],
        out_specs=(vmem, vmem, vmem, vmem),
        scratch_shapes=[pltpu.VMEM((2, 2 * span, depth), BF16),
                        pltpu.VMEM((lines, 2, width, 2 * span), BF16),
                        pltpu.VMEM((blocks, width, 2 * span), BF16),
                        pltpu.VMEM((1, depth), F32),
                        pltpu.VMEM((blocks, span, max(8, 2 * heads)), F32),
                        pltpu.VMEM((blocks, width, span), F32),
                        pltpu.VMEM((blocks, width, span), F32),
                        pltpu.VMEM((blocks, 2, width, span), BF16),
                        pltpu.VMEM((blocks, width, span), BF16),
                        pltpu.VMEM((blocks, 2, width, span), BF16),
                        pltpu.VMEM((blocks, width, span), BF16),
                        pltpu.VMEM((blocks, 2 * span + 16, width), BF16),
                        pltpu.VMEM((blocks, span, width), BF16),
                        pltpu.VMEM((span, depth), F32),
                        pltpu.VMEM((blocks, depth, width), BF16),
                        pltpu.VMEM((blocks, 8, span), F32),
                        pltpu.VMEM((ndp, 8, span), F32),
                        sem((3,)), sem((2,)), sem((2,)), sem((2 + ndp, blocks)), sem((ndp, blocks)),
                        sem((lines, 2)), sem((blocks,)), sem((blocks,)), sem((blocks,)), sem((blocks,)),
                        sem((blocks,)), sem((blocks,)), sem((blocks,)), sem((ndp,)), sem((ndp,))],
        compiler_params=pltpu.CompilerParams(collective_id=0, has_side_effects=True,
                                             vmem_limit_bytes=56 * 1024 * 1024),
        name="layer",
    )(tokens, probe_rows, w_query, sharpness, pattern, lengths, start_vector.reshape(1, depth))


def keep_kernel(scale_term, scale_sharp, a_ref, b_ref, stat_ref, spec_ref, len_ref, a_out, b_out, term_out,
                sharp_out, spec_out, norm_out):
    a_out[...] = a_ref[...]
    b_out[...] = b_ref[...]
    spec_out[...] = spec_ref[...]
    span = stat_ref.shape[1]
    row_at = lax.broadcasted_iota(jnp.int32, (8, span), 0)
    column_at = lax.broadcasted_iota(jnp.int32, (8, span), 1)

    def as_row(at):
        return jnp.sum(jnp.where(row_at == column_at, stat_ref[at:at + 8], 0.0), axis=0, keepdims=True)

    count = jnp.full((1, span), len_ref[0], jnp.int32).astype(F32) * scale_term
    term_out[...] = (as_row(0) / count)[:, :term_out.shape[1]]
    sharp_out[...] = (as_row(8) * scale_sharp)[:, :sharp_out.shape[1]]
    norm_out[...] = stat_ref[16:17, :1]


def keep(a, b, stats, spec, lengths, heads, scale_term, scale_sharp):
    smem = pl.BlockSpec(memory_space=pltpu.SMEM)
    vmem = pl.BlockSpec(memory_space=pltpu.VMEM)
    return pl.pallas_call(
        functools.partial(keep_kernel, scale_term, scale_sharp),
        out_shape=(jax.ShapeDtypeStruct(a.shape, a.dtype), jax.ShapeDtypeStruct(b.shape, b.dtype),
                   jax.ShapeDtypeStruct((1, 2), F32), jax.ShapeDtypeStruct((1, heads), F32),
                   jax.ShapeDtypeStruct(spec.shape, F32), jax.ShapeDtypeStruct((1, 1), F32)),
        in_specs=[vmem, vmem, vmem, vmem, smem],
        out_specs=(vmem,) * 6, name="keep")(a, b, stats, spec, lengths)


def shards(inputs, w_query, sharpness, pattern, lengths, probes, start_vector):
    tokens = inputs[0]
    probe_rows = probes[0]
    rows_here = tokens.shape[0]
    groups = lax.axis_size("seq")
    inner_here = w_query.shape[1]
    inner = inner_here * groups
    branch, probe_vjp, stats, spec = layer(
        lax.axis_size("dp"), groups, tokens, probe_rows, w_query, sharpness, pattern.T, lengths, start_vector)
    heads = sharpness.shape[0]
    scale_sharp = -1.0 / math.sqrt(DH) / (lax.axis_size("dp") * groups * rows_here * DH)
    branch, probe_vjp, terms, sharp_grad, spec, norm = keep(
        branch, probe_vjp, stats, spec, lengths, heads, float(inner), scale_sharp)
    return (branch[None], probe_vjp[None], terms, sharp_grad.reshape(-1), spec.reshape(-1), norm.reshape(-1))


def solution(mesh):
    placed = (
        P("dp", "seq", None),
        P(None, "seq"),
        P("seq"),
        P(),
        P("dp"),
        P("dp", "seq", None),
        P(),
    )
    return jax.shard_map(
        shards,
        mesh=mesh,
        in_specs=placed,
        out_specs=(P("dp", "seq", None), P("dp", "seq", None), P("dp", None), P("seq"), P(), P()),
        check_vma=False,
    )
```

```python
import functools
import math

import jax
import jax.numpy as jnp
from jax import lax
from jax.experimental import pallas as pl
from jax.experimental.pallas import tpu as pltpu
from jax.sharding import PartitionSpec as P

DH = 64
F32 = jnp.float32
BF16 = jnp.bfloat16


def dot(a, b, ca, cb):
    return lax.dot_general(a, b, (((ca,), (cb,)), ((), ())), preferred_element_type=F32)


def layer_kernel(heads, ndp, x_ref, p_ref, w_ref, sharp_ref, pat_ref, len_ref, start_ref, branch_ref,
                 vjp_ref, stat_ref, spec_ref, both, outbox, qc_refs, image, cols, own, other_part, box_a, box_g,
                 home_a, home_g, left_rows, grad_rows, adjoint_out, w_all, seq_tile, dp_tile, loc_sem, x_send,
                 x_recv, w_send, w_recv, q_send, q_recv, a_send, a_recv, g_send, g_recv, s_send, s_recv, d_send,
                 d_recv):
    blocks, depth, width = w_all.shape
    pair = both.shape[1]
    span = pair // 2
    lines, ys, rows = blocks // 2, ndp // 2, depth // ndp
    cuts = max(1, width // 128)
    part_width = width // cuts
    me, d = lax.axis_index("seq"), lax.axis_index("dp")
    z, x = me // 2, me % 2
    y, core = d // 2, d % 2
    mate_d = d + 1 - 2 * core
    beside = me + 1 - 2 * x
    length = len_ref[0]
    mesh_id = pl.DeviceIdType.MESH

    loads = [pltpu.make_async_copy(w_ref, w_all.at[me], loc_sem.at[0]),
             pltpu.make_async_copy(x_ref, both.at[x, :span], loc_sem.at[1]),
             pltpu.make_async_copy(p_ref, both.at[x, span:], loc_sem.at[2])]
    for load in loads:
        load.start()
    barrier = pltpu.get_barrier_semaphore()
    for k in range(1, blocks):
        pl.semaphore_signal(barrier, inc=1, device_id={"seq": (me + k) % blocks, "dp": d},
                            device_id_type=mesh_id)
    for k in range(1, ndp):
        pl.semaphore_signal(barrier, inc=1, device_id={"seq": me, "dp": (d + k) % ndp},
                            device_id_type=mesh_id)
    pl.semaphore_wait(barrier, blocks + ndp - 2)

    def push(src, dst, send, recv, target, t_dp):
        return pltpu.make_async_remote_copy(
            src_ref=src, dst_ref=dst, send_sem=send, recv_sem=recv,
            device_id={"seq": target, "dp": t_dp}, device_id_type=mesh_id)

    def push_a(i, c):
        return push(box_a.at[i, c], home_a.at[me, c], a_send.at[i, c], a_recv.at[me, c], i, d)

    def push_g(i, c):
        return push(box_g.at[i, c], home_g.at[me, c], g_send.at[i, c], g_recv.at[me, c], i, d)

    def push_s(i):
        return push(seq_tile.at[me], seq_tile.at[me], s_send.at[i], s_recv.at[me], i, d)

    def push_d(j):
        return push(dp_tile.at[d], dp_tile.at[d], d_send.at[j], d_recv.at[d], me, j)

    def arrived(ref, sem):
        pltpu.make_async_copy(ref, ref, sem).wait()

    def push_x():
        return push(x_ref, both.at[x, :span], x_send.at[0], x_recv.at[0], beside, d)

    def push_p():
        return push(p_ref, both.at[x, span:], x_send.at[1], x_recv.at[1], beside, d)

    def part(owner):
        return pl.ds(pl.multiple_of(owner * rows, rows), rows)

    def cut_at(c):
        return slice(c * part_width, (c + 1) * part_width)

    def piece(s, c, owner, kind, target, t_dp, first=False):
        here = w_all.at[s, part(owner), cut_at(c)]
        src = w_ref.at[part(owner), cut_at(c)] if first else here
        at = s * cuts + c
        return push(src, here, w_send.at[kind, at], w_recv.at[owner, at], target, t_dp)

    def landed(s, c, owner):
        arrived(w_all.at[s, part(owner), cut_at(c)], w_recv.at[owner, s * cuts + c])

    up, down = (me + 2) % blocks, (me + blocks - 2) % blocks

    def line(t):
        m = jnp.minimum(z, lines - 1 - z)
        near = jnp.where(t % 2 == 1, z + (t + 1) // 2, z - t // 2)
        far = jnp.where(2 * z < lines, t, lines - 1 - t)
        return jnp.where(t <= 2 * m, near, far)

    def spread(s, c):
        for k in range(1, ys):
            piece(s, c, d, 3 + k, me, ((y + k) % ys) * 2 + core).start()
        piece(s, c, d, 3, me, mate_d).start()

    def relay(s, c):
        for k in range(1, ys):
            owner = ((y + k) % ys) * 2 + core
            landed(s, c, owner)
            piece(s, c, owner, 2 + ys + k, me, mate_d).start()

    def complete(s, c):
        for k in range(ys):
            landed(s, c, ((y + k) % ys) * 2 + 1 - core)

    def spread_done(s, c):
        for k in range(1, ys):
            piece(s, c, d, 3 + k, me, d).wait_send()
            piece(s, c, d, 2 + ys + k, me, d).wait_send()
        piece(s, c, d, 3, me, d).wait_send()

    def forward(t, c):
        at = line(t)
        s = at * 2 + x
        landed(s, c, d)
        pl.when((at < z) & (z + 1 < lines))(lambda: piece(s, c, d, 0, up, d).start())
        pl.when((at > z) & (z > 0))(lambda: piece(s, c, d, 1, down, d).start())
        spread(s, c)

    def own_piece(c):
        pl.when(z + 1 < lines)(lambda: piece(me, c, d, 0, up, d, True).start())
        pl.when(z > 0)(lambda: piece(me, c, d, 1, down, d, True).start())

    own_piece(0)
    push_x().start()
    push_p().start()
    token_at = lax.broadcasted_iota(jnp.int32, (1, span), 1)

    def project(s, side, c):
        res = jnp.transpose(dot(both[side], w_all[s, :, cut_at(c)], 1, 0))
        kept = jnp.concatenate([token_at >= 0, (z * 2 + side) * span + token_at < length], axis=1)
        return jnp.where(kept, res, 0.0).astype(BF16)

    def push_q(at, side, c):
        block_at = z * 2 + side
        return push(outbox.at[at, side, cut_at(c)], qc_refs[c].at[block_at], q_send.at[at, side, c],
                    q_recv.at[block_at, c], at * 2 + x, d)

    for load in loads:
        load.wait()
    for c in range(cuts):
        qc_refs[c][me] = project(me, x, c)

    def first_product(t, c):
        at = line(t)
        s = at * 2 + x
        relay(s, c)
        complete(s, c)
        outbox[at, x, cut_at(c)] = project(s, x, c)
        push_q(at, x, c).start()

    lag = jnp.where((z > 0) & (z + 1 < lines), 2, 1)
    for c in range(cuts):

        def tick(t, carry):
            forward(t, c)
            if c + 1 < cuts:
                pl.when(t == jnp.minimum(lag, 2))(lambda: own_piece(c + 1))
            pl.when(t > lag)(lambda: first_product(t - lag, c))
            if c > 0:
                pl.when((t <= lag) & (t + lines - 1 > lag))(lambda: first_product(t + lines - 1 - lag, c - 1))
            return carry

        lax.fori_loop(1, lines, tick, 0)

    def rest(t, carry):
        pl.when(t + lag >= lines)(lambda: first_product(t, cuts - 1))
        return carry

    lax.fori_loop(1, lines, rest, 0)

    def across(t, carry):
        for c in range(cuts):
            piece(line(t) * 2 + x, c, d, 2, beside, d).start()
        return carry

    lax.fori_loop(0, lines, across, 0)
    arrived(both.at[1 - x, :span], x_recv.at[0])
    arrived(both.at[1 - x, span:], x_recv.at[1])
    for c in range(cuts):

        def partner(t, carry):
            at = line(t)
            outbox[at, 1 - x, cut_at(c)] = project(at * 2 + x, 1 - x, c)
            push_q(at, 1 - x, c).start()
            return carry

        lax.fori_loop(1, lines, partner, 0)
        qc_refs[c][beside] = project(me, 1 - x, c)

    def spread_other(t):
        for c in range(cuts):
            s = line(t) * 2 + 1 - x
            landed(s, c, d)
            spread(s, c)

    def relay_other(t):
        for c in range(cuts):
            relay(line(t) * 2 + 1 - x, c)

    spread_other(0)
    per_cut = heads // cuts

    def prepare(c, k, carry):
        i = (me - x + k) % blocks
        pl.when(k > 1)(lambda: arrived(qc_refs[c].at[i], q_recv.at[i, c]))
        q = qc_refs[c][i, :, :span].astype(F32)
        r = qc_refs[c][i, :, span:].astype(F32)
        rows = [jnp.sum((q * q)[h * DH:(h + 1) * DH], axis=0, keepdims=True) for h in range(per_cut)]
        rows += [jnp.sum((q * r)[h * DH:(h + 1) * DH], axis=0, keepdims=True) for h in range(per_cut)]
        if 2 * per_cut < 8:
            rows.append(jnp.zeros((8 - 2 * per_cut, span), F32))
        cols[c, i] = jnp.transpose(jnp.concatenate(rows, axis=0))
        return carry

    sharp_at = dp_tile.at[d]
    sharp_at[...] = jnp.zeros((8, span), F32)
    key_at = lax.broadcasted_iota(jnp.int32, (span, span), 0)
    query_at = lax.broadcasted_iota(jnp.int32, (span, span), 1)
    tail = (lax.broadcasted_iota(jnp.int32, (16, 2 * span), 1) < span).astype(F32).astype(BF16)

    def block(cut, k, carry):
        i = (me + blocks // 2 + k) % blocks
        other = pat_ref[1, i]
        allowed = jnp.concatenate(
            [(i * span + key_at < length) | (key_at == query_at), other * span + key_at < length],
            axis=0)
        for n in range(per_cut):
            h = cut * per_cut + n
            hs = slice(h * DH, (h + 1) * DH)
            ns = slice(n * DH, (n + 1) * DH)
            qc = qc_refs[cut][i, ns, :]
            qc_other = qc_refs[cut][other, ns, :]
            q = qc[:, :span]
            c = qc[:, span:]
            keys = jnp.concatenate([q, qc_other[:, :span]], axis=1)
            key_cots = jnp.concatenate([c, qc_other[:, span:]], axis=1)
            both = dot(keys, qc, 0, 0)
            inner = both[:, :span]
            prob_grad = both[:, span:]
            cross = dot(key_cots, q, 0, 0)
            qf = q.astype(F32)
            cf = c.astype(F32)
            norm_row = jnp.sum(qf * qf, axis=0, keepdims=True)
            pair_row = jnp.sum(qf * cf, axis=0, keepdims=True)
            norm_col = jnp.concatenate([cols[cut, i, :, n:n + 1], cols[cut, other, :, n:n + 1]], axis=0)
            pair_col = jnp.concatenate(
                [cols[cut, i, :, per_cut + n:per_cut + n + 1], cols[cut, other, :, per_cut + n:per_cut + n + 1]],
                axis=0)
            factor = sharp_ref[h] * (1.0 / math.sqrt(DH))
            distance = norm_row + norm_col - 2.0 * inner
            weights = jnp.where(allowed, jnp.exp(-factor * distance), 0.0)
            total = jnp.sum(weights, axis=0, keepdims=True)
            soft = weights * (1.0 / total)
            low = soft.astype(BF16)
            row_inner = jnp.sum(soft * prob_grad, axis=0, keepdims=True)
            score = soft * (prob_grad - row_inner)
            dp_tile[d, h:h + 1, :] += jnp.sum(score * distance, axis=0, keepdims=True)
            coef = (-2.0 * factor * score).astype(BF16)
            row_total = jnp.sum(coef.astype(F32), axis=0, keepdims=True)
            gap = pair_row + pair_col - cross - prob_grad
            gap_mean = jnp.sum(soft * gap, axis=0, keepdims=True)
            adj = (-2.0 * factor * (soft * (gap - gap_mean))).astype(BF16)
            mixed = jnp.concatenate([coef, low], axis=1)
            left = dot(keys, mixed, 1, 0)
            box_a[i, cut, 0, ns, :] = left[:, span:].astype(BF16)
            adjoint = dot(jnp.concatenate([keys, key_cots], axis=1),
                          jnp.concatenate([adj, low], axis=0), 1, 0)
            box_a[i, cut, 1, ns, :] = adjoint.astype(BF16)
            lhs = jnp.concatenate([jnp.concatenate([-q, c], axis=1), tail], axis=0)
            right = dot(lhs, mixed, 1, 1)
            key_part = keys.astype(F32) * right[DH:DH + 1, :] + right[:DH]
            own[i, hs, :] = qf * row_total - left[:, :span] + key_part[:, :span]
            other_part[i, hs, :] = key_part[:, span:]
        pl.when(i != me)(lambda: push_a(i, cut).start())
        if cut + 1 == cuts:

            @pl.when(k % 2 == 1)
            def _():
                pl.when(2 + k // 2 < lines)(lambda: spread_other(2 + k // 2))
                pl.when(1 + k // 2 < lines)(lambda: relay_other(1 + k // 2))

        return carry

    def finish(cut, k, term):
        m = (me + blocks // 2 + k) % blocks
        at = cut_at(cut)

        def gather(i, total):
            chosen = jnp.where(pat_ref[1, i] == m, 1.0, 0.0)
            return total + other_part[i, at] * chosen

        if blocks <= 8:
            g = own[m, at]
            for i in range(blocks):
                g = gather(i, g)
        else:
            g = lax.fori_loop(0, blocks, gather, own[m, at])
        box_g[m, cut] = g.astype(BF16)
        pl.when(m != me)(lambda: push_g(m, cut).start())
        return term + jnp.sum(g * qc_refs[cut][m, :, span:].astype(F32), axis=0, keepdims=True)

    term_one = jnp.zeros((1, span), F32)
    for cut in range(cuts):
        lax.fori_loop(0, blocks, functools.partial(prepare, cut), 0)
        if cut + 1 == cuts:
            spread_other(1)
            relay_other(0)
        lax.fori_loop(0, blocks, functools.partial(block, cut), 0)
        term_one = lax.fori_loop(0, blocks, functools.partial(finish, cut), term_one)
    for k in range(1, ndp):
        push_d((d + k) % ndp).start()
    home_a[me] = box_a[me]
    home_g[me] = box_g[me]

    def whole(t, carry):
        for c in range(cuts):
            complete(line(t) * 2 + 1 - x, c)
        return carry

    lax.fori_loop(0, lines, whole, 0)

    def take_a(k, carry):
        s = (me + k) % blocks
        for c in range(cuts):
            pl.when(k > 0)(lambda: arrived(home_a.at[s, c], a_recv.at[s, c]))
            left_rows[s, :2 * span, cut_at(c)] = jnp.concatenate(
                [jnp.transpose(home_a[s, c, 0]), jnp.transpose(home_a[s, c, 1])], axis=0)
        return carry

    def split(v):
        high = v.astype(BF16).astype(F32)
        mid = (v - high).astype(BF16).astype(F32)
        rows = [high, mid, v - high - mid, jnp.zeros((13, v.shape[1]), F32)]
        return jnp.concatenate(rows, axis=0).astype(BF16)

    start_rows = split(start_ref[...])

    def power(s, total):
        column = jnp.sum(dot(start_rows, w_all[s], 1, 0), axis=0, keepdims=True)
        left_rows[s, 2 * span:, :] = split(column)
        return total + column * column

    column_sq = lax.fori_loop(0, blocks, power, jnp.zeros((1, width), F32))
    lax.fori_loop(0, blocks, take_a, 0)
    step = 256

    def product(rows_ref, r):
        at = pl.ds(pl.multiple_of(r * step, step), step)
        total = jnp.zeros((rows_ref.shape[1], step), F32)
        for s in range(blocks):
            total = total + dot(rows_ref[s], w_all[s, at, :], 1, 1)
        return at, total

    def outward(r, carry):
        at, total = product(left_rows, r)
        branch_ref[:, at] = total[:span].astype(BF16)
        adjoint_out[:, at] = total[span:2 * span]
        image[:, at] = jnp.sum(total[2 * span:], axis=0, keepdims=True)
        return carry

    lax.fori_loop(0, depth // step, outward, 0)

    def take_g(k, carry):
        s = (me + k) % blocks
        for c in range(cuts):
            pl.when(k > 0)(lambda: arrived(home_g.at[s, c], g_recv.at[s, c]))
            grad_rows[s, :, cut_at(c)] = jnp.transpose(home_g[s, c])
        return carry

    lax.fori_loop(0, blocks, take_g, 0)

    def backward(r, term):
        at, total = product(grad_rows, r)
        low = total.astype(BF16)
        vjp_ref[:, at] = low
        part = low.astype(F32) * adjoint_out[:, at]
        for n in range(step // span):
            term = term + jnp.sum(part[:, n * span:(n + 1) * span], axis=0, keepdims=True)
        return term

    image_sq = jnp.sum(image[...] * image[...], axis=1, keepdims=True)
    spec_ref[...] = image[...] / jnp.sqrt(image_sq / depth + 1e-06)
    norm = jnp.sqrt(image_sq / (jnp.sum(column_sq, axis=1, keepdims=True) + 1e-06))
    stat_ref[16:] = jnp.broadcast_to(norm, (8, span))
    term_two = lax.fori_loop(0, depth // step, backward, jnp.zeros((1, span), F32))
    seq_tile[me] = jnp.concatenate([term_one, term_two, jnp.zeros((6, span), F32)], axis=0)
    for k in range(1, blocks):
        push_s((me + k) % blocks).start()
    for k in range(1, ndp):
        j = (d + k) % ndp
        arrived(dp_tile.at[j], d_recv.at[j])
        push_d(j).wait_send()
    for k in range(1, blocks):
        i = (me + k) % blocks
        for c in range(cuts):
            push_a(i, c).wait_send()
            push_g(i, c).wait_send()
        arrived(seq_tile.at[i], s_recv.at[i])
        push_s(i).wait_send()
    push_x().wait_send()
    push_p().wait_send()

    def drain(t, carry):
        at = line(t)
        s = at * 2 + x
        for c in range(cuts):
            pl.when((at <= z) & (z + 1 < lines))(lambda: piece(s, c, d, 0, up, d).wait_send())
            pl.when((at >= z) & (z > 0))(lambda: piece(s, c, d, 1, down, d).wait_send())
            piece(s, c, d, 2, beside, d).wait_send()
            spread_done(at * 2 + 1 - x, c)

        @pl.when(t > 0)
        def _():
            for c in range(cuts):
                spread_done(s, c)
            for c in range(cuts):
                push_q(at, 0, c).wait_send()
                push_q(at, 1, c).wait_send()

        return carry

    lax.fori_loop(0, lines, drain, 0)
    stat_ref[:8] = jnp.broadcast_to(
        jnp.sum(jnp.sum(seq_tile[...], axis=0), axis=1, keepdims=True), (8, span))
    stat_ref[8:16] = jnp.broadcast_to(
        jnp.sum(jnp.sum(dp_tile[...], axis=0), axis=1, keepdims=True), (8, span))


def layer(ndp, groups, tokens, probe_rows, w_query, sharpness, pattern, lengths, start_vector):
    span, depth = tokens.shape
    width = w_query.shape[1]
    blocks, lines = groups, groups // 2
    cuts = max(1, width // 128)
    heads = sharpness.shape[0]
    smem = pl.BlockSpec(memory_space=pltpu.SMEM)
    vmem = pl.BlockSpec(memory_space=pltpu.VMEM)
    hbm = pl.BlockSpec(memory_space=pl.ANY)
    sem = pltpu.SemaphoreType.DMA
    return pl.pallas_call(
        functools.partial(layer_kernel, heads, ndp),
        out_shape=(jax.ShapeDtypeStruct((span, depth), BF16),
                   jax.ShapeDtypeStruct((span, depth), BF16),
                   jax.ShapeDtypeStruct((24, span), F32),
                   jax.ShapeDtypeStruct((1, depth), F32)),
        in_specs=[hbm, hbm, hbm, smem, smem, smem, vmem],
        out_specs=(vmem, vmem, vmem, vmem),
        scratch_shapes=[pltpu.VMEM((2, 2 * span, depth), BF16),
                        pltpu.VMEM((lines, 2, width, 2 * span), BF16),
                        [pltpu.VMEM((blocks, width // cuts, 2 * span), BF16)] * cuts,
                        pltpu.VMEM((1, depth), F32),
                        pltpu.VMEM((cuts, blocks, span, max(8, 2 * heads // cuts)), F32),
                        pltpu.VMEM((blocks, width, span), F32),
                        pltpu.VMEM((blocks, width, span), F32),
                        pltpu.VMEM((blocks, cuts, 2, width // cuts, span), BF16),
                        pltpu.VMEM((blocks, cuts, width // cuts, span), BF16),
                        pltpu.VMEM((blocks, cuts, 2, width // cuts, span), BF16),
                        pltpu.VMEM((blocks, cuts, width // cuts, span), BF16),
                        pltpu.VMEM((blocks, 2 * span + 16, width), BF16),
                        pltpu.VMEM((blocks, span, width), BF16),
                        pltpu.VMEM((span, depth), F32),
                        pltpu.VMEM((blocks, depth, width), BF16),
                        pltpu.VMEM((blocks, 8, span), F32),
                        pltpu.VMEM((ndp, 8, span), F32),
                        sem((3,)), sem((2,)), sem((2,)), sem((2 + ndp, blocks * cuts)), sem((ndp, blocks * cuts)),
                        sem((lines, 2, cuts)), sem((blocks, cuts)), sem((blocks, cuts)), sem((blocks, cuts)),
                        sem((blocks, cuts)), sem((blocks, cuts)), sem((blocks,)), sem((blocks,)), sem((ndp,)),
                        sem((ndp,))],
        compiler_params=pltpu.CompilerParams(collective_id=0, has_side_effects=True,
                                             vmem_limit_bytes=56 * 1024 * 1024),
        name="layer",
    )(tokens, probe_rows, w_query, sharpness, pattern, lengths, start_vector.reshape(1, depth))


def keep_kernel(scale_term, scale_sharp, a_ref, b_ref, stat_ref, spec_ref, len_ref, a_out, b_out, term_out,
                sharp_out, spec_out, norm_out):
    a_out[...] = a_ref[...]
    b_out[...] = b_ref[...]
    spec_out[...] = spec_ref[...]
    span = stat_ref.shape[1]
    row_at = lax.broadcasted_iota(jnp.int32, (8, span), 0)
    column_at = lax.broadcasted_iota(jnp.int32, (8, span), 1)

    def as_row(at):
        return jnp.sum(jnp.where(row_at == column_at, stat_ref[at:at + 8], 0.0), axis=0, keepdims=True)

    count = jnp.full((1, span), len_ref[0], jnp.int32).astype(F32) * scale_term
    term_out[...] = (as_row(0) / count)[:, :term_out.shape[1]]
    sharp_out[...] = (as_row(8) * scale_sharp)[:, :sharp_out.shape[1]]
    norm_out[...] = stat_ref[16:17, :1]


def keep(a, b, stats, spec, lengths, heads, scale_term, scale_sharp):
    smem = pl.BlockSpec(memory_space=pltpu.SMEM)
    vmem = pl.BlockSpec(memory_space=pltpu.VMEM)
    return pl.pallas_call(
        functools.partial(keep_kernel, scale_term, scale_sharp),
        out_shape=(jax.ShapeDtypeStruct(a.shape, a.dtype), jax.ShapeDtypeStruct(b.shape, b.dtype),
                   jax.ShapeDtypeStruct((1, 2), F32), jax.ShapeDtypeStruct((1, heads), F32),
                   jax.ShapeDtypeStruct(spec.shape, F32), jax.ShapeDtypeStruct((1, 1), F32)),
        in_specs=[vmem, vmem, vmem, vmem, smem],
        out_specs=(vmem,) * 6, name="keep")(a, b, stats, spec, lengths)


def shards(inputs, w_query, sharpness, pattern, lengths, probes, start_vector):
    tokens = inputs[0]
    probe_rows = probes[0]
    rows_here = tokens.shape[0]
    groups = lax.axis_size("seq")
    inner_here = w_query.shape[1]
    inner = inner_here * groups
    branch, probe_vjp, stats, spec = layer(
        lax.axis_size("dp"), groups, tokens, probe_rows, w_query, sharpness, pattern.T, lengths, start_vector)
    heads = sharpness.shape[0]
    scale_sharp = -1.0 / math.sqrt(DH) / (lax.axis_size("dp") * groups * rows_here * DH)
    branch, probe_vjp, terms, sharp_grad, spec, norm = keep(
        branch, probe_vjp, stats, spec, lengths, heads, float(inner), scale_sharp)
    return (branch[None], probe_vjp[None], terms, sharp_grad.reshape(-1), spec.reshape(-1), norm.reshape(-1))


def solution(mesh):
    placed = (
        P("dp", "seq", None),
        P(None, "seq"),
        P("seq"),
        P(),
        P("dp"),
        P("dp", "seq", None),
        P(),
    )
    return jax.shard_map(
        shards,
        mesh=mesh,
        in_specs=placed,
        out_specs=(P("dp", "seq", None), P("dp", "seq", None), P("dp", None), P("seq"), P(), P()),
        check_vma=False,
    )
```

```python
import functools
import math

import jax
import jax.numpy as jnp
from jax import lax
from jax.experimental import pallas as pl
from jax.experimental.pallas import tpu as pltpu
from jax.sharding import PartitionSpec as P

DH = 64
F32 = jnp.float32
BF16 = jnp.bfloat16


def dot(a, b, ca, cb):
    return lax.dot_general(a, b, (((ca,), (cb,)), ((), ())), preferred_element_type=F32)


def layer_kernel(heads, ndp, x_ref, p_ref, w_ref, sharp_ref, pat_ref, len_ref, start_ref, branch_ref,
                 vjp_ref, stat_ref, spec_ref, both, outbox, qc_refs, image, cols, own, other_part, box_a, box_g,
                 home_a, home_g, left_rows, grad_rows, adjoint_out, w_all, seq_tile, dp_tile, loc_sem, x_send,
                 x_recv, w_send, w_recv, q_send, q_recv, a_send, a_recv, g_send, g_recv, s_send, s_recv, d_send,
                 d_recv):
    blocks, depth, width = w_all.shape
    pair = both.shape[1]
    span = pair // 2
    lines, ys, rows = blocks // 2, ndp // 2, depth // ndp
    cuts = max(1, width // 128)
    part_width = width // cuts
    me, d = lax.axis_index("seq"), lax.axis_index("dp")
    z, x = me // 2, me % 2
    y, core = d // 2, d % 2
    mate_d = d + 1 - 2 * core
    beside = me + 1 - 2 * x
    length = len_ref[0]
    mesh_id = pl.DeviceIdType.MESH

    loads = [pltpu.make_async_copy(w_ref, w_all.at[me], loc_sem.at[0]),
             pltpu.make_async_copy(x_ref, both.at[x, :span], loc_sem.at[1]),
             pltpu.make_async_copy(p_ref, both.at[x, span:], loc_sem.at[2])]
    for load in loads:
        load.start()
    barrier = pltpu.get_barrier_semaphore()
    for k in range(1, blocks):
        pl.semaphore_signal(barrier, inc=1, device_id={"seq": (me + k) % blocks, "dp": d},
                            device_id_type=mesh_id)
    for k in range(1, ndp):
        pl.semaphore_signal(barrier, inc=1, device_id={"seq": me, "dp": (d + k) % ndp},
                            device_id_type=mesh_id)
    pl.semaphore_wait(barrier, blocks + ndp - 2)

    def push(src, dst, send, recv, target, t_dp):
        return pltpu.make_async_remote_copy(
            src_ref=src, dst_ref=dst, send_sem=send, recv_sem=recv,
            device_id={"seq": target, "dp": t_dp}, device_id_type=mesh_id)

    def push_a(i, c):
        return push(box_a.at[i, c], home_a.at[me, c], a_send.at[i, c], a_recv.at[me, c], i, d)

    def push_g(i, c):
        return push(box_g.at[i, c], home_g.at[me, c], g_send.at[i, c], g_recv.at[me, c], i, d)

    def push_s(i):
        return push(seq_tile.at[me], seq_tile.at[me], s_send.at[i], s_recv.at[me], i, d)

    def push_d(j):
        return push(dp_tile.at[d], dp_tile.at[d], d_send.at[j], d_recv.at[d], me, j)

    def arrived(ref, sem):
        pltpu.make_async_copy(ref, ref, sem).wait()

    def push_x():
        return push(x_ref, both.at[x, :span], x_send.at[0], x_recv.at[0], beside, d)

    def push_p():
        return push(p_ref, both.at[x, span:], x_send.at[1], x_recv.at[1], beside, d)

    def part(owner):
        return pl.ds(pl.multiple_of(owner * rows, rows), rows)

    def cut_at(c):
        return slice(c * part_width, (c + 1) * part_width)

    def piece(s, c, owner, kind, target, t_dp, first=False):
        here = w_all.at[s, part(owner), cut_at(c)]
        src = w_ref.at[part(owner), cut_at(c)] if first else here
        at = s * cuts + c
        return push(src, here, w_send.at[kind, at], w_recv.at[owner, at], target, t_dp)

    def landed(s, c, owner):
        arrived(w_all.at[s, part(owner), cut_at(c)], w_recv.at[owner, s * cuts + c])

    up, down = (me + 2) % blocks, (me + blocks - 2) % blocks

    def line(t):
        m = jnp.minimum(z, lines - 1 - z)
        near = jnp.where(t % 2 == 1, z + (t + 1) // 2, z - t // 2)
        far = jnp.where(2 * z < lines, t, lines - 1 - t)
        return jnp.where(t <= 2 * m, near, far)

    def spread(s, c):
        for k in range(1, ys):
            piece(s, c, d, 3 + k, me, ((y + k) % ys) * 2 + core).start()
        piece(s, c, d, 3, me, mate_d).start()

    def relay(s, c):
        for k in range(1, ys):
            owner = ((y + k) % ys) * 2 + core
            landed(s, c, owner)
            piece(s, c, owner, 2 + ys + k, me, mate_d).start()

    def complete(s, c):
        for k in range(ys):
            landed(s, c, ((y + k) % ys) * 2 + 1 - core)

    def spread_done(s, c):
        for k in range(1, ys):
            piece(s, c, d, 3 + k, me, d).wait_send()
            piece(s, c, d, 2 + ys + k, me, d).wait_send()
        piece(s, c, d, 3, me, d).wait_send()

    def forward(t, c):
        at = line(t)
        s = at * 2 + x
        landed(s, c, d)
        pl.when((at < z) & (z + 1 < lines))(lambda: piece(s, c, d, 0, up, d).start())
        pl.when((at > z) & (z > 0))(lambda: piece(s, c, d, 1, down, d).start())
        spread(s, c)
        piece(s, c, d, 2, beside, d).start()

    def own_piece(c):
        pl.when(z + 1 < lines)(lambda: piece(me, c, d, 0, up, d, True).start())
        pl.when(z > 0)(lambda: piece(me, c, d, 1, down, d, True).start())

    own_piece(0)
    push_x().start()
    push_p().start()
    for c in range(cuts):
        piece(me, c, d, 2, beside, d, True).start()
    token_at = lax.broadcasted_iota(jnp.int32, (1, span), 1)

    def project(s, side, c):
        res = jnp.transpose(dot(both[side], w_all[s, :, cut_at(c)], 1, 0))
        kept = jnp.concatenate([token_at >= 0, (z * 2 + side) * span + token_at < length], axis=1)
        return jnp.where(kept, res, 0.0).astype(BF16)

    def push_q(at, side, c):
        block_at = z * 2 + side
        return push(outbox.at[at, side, cut_at(c)], qc_refs[c].at[block_at], q_send.at[at, side, c],
                    q_recv.at[block_at, c], at * 2 + x, d)

    for load in loads:
        load.wait()
    for c in range(cuts):
        qc_refs[c][me] = project(me, x, c)

    def first_product(t, c):
        at = line(t)
        s = at * 2 + x
        relay(s, c)
        complete(s, c)
        outbox[at, x, cut_at(c)] = project(s, x, c)
        push_q(at, x, c).start()

    lag = jnp.where((z > 0) & (z + 1 < lines), 2, 1)
    for c in range(cuts):

        def tick(t, carry):
            forward(t, c)
            if c + 1 < cuts:
                pl.when(t == jnp.minimum(lag, 2))(lambda: own_piece(c + 1))
            pl.when(t > lag)(lambda: first_product(t - lag, c))
            if c > 0:
                pl.when((t <= lag) & (t + lines - 1 > lag))(lambda: first_product(t + lines - 1 - lag, c - 1))
            return carry

        lax.fori_loop(1, lines, tick, 0)

    def rest(t, carry):
        pl.when(t + lag >= lines)(lambda: first_product(t, cuts - 1))
        return carry

    lax.fori_loop(1, lines, rest, 0)

    arrived(both.at[1 - x, :span], x_recv.at[0])
    arrived(both.at[1 - x, span:], x_recv.at[1])
    for c in range(cuts):

        def partner(t, carry):
            at = line(t)
            outbox[at, 1 - x, cut_at(c)] = project(at * 2 + x, 1 - x, c)
            push_q(at, 1 - x, c).start()
            return carry

        lax.fori_loop(1, lines, partner, 0)
        qc_refs[c][beside] = project(me, 1 - x, c)

    units = [(0, c) for c in range(cuts)] + [(t, c) for c in range(cuts) for t in range(1, lines)]

    def spread_other(g):
        for t, c in units[g * cuts:(g + 1) * cuts]:
            s = line(t) * 2 + 1 - x
            landed(s, c, d)
            spread(s, c)

    def relay_other(g):
        for t, c in units[g * cuts:(g + 1) * cuts]:
            relay(line(t) * 2 + 1 - x, c)

    total_steps = cuts * blocks
    stride = max(1, (total_steps - 2) // max(1, lines - 2))
    events = [(4 + stride * (g - 2), 0, g) for g in range(2, lines)]
    events += [(5 + (stride + 1) * (g - 1), 1, g) for g in range(1, lines)]
    events.sort()

    def run_event(event):
        (relay_other if event[1] else spread_other)(event[2])

    spread_other(0)
    spread_other(1)
    relay_other(0)
    per_cut = heads // cuts

    def prepare(c, k, carry):
        i = (me - x + k) % blocks
        pl.when(k > 1)(lambda: arrived(qc_refs[c].at[i], q_recv.at[i, c]))
        q = qc_refs[c][i, :, :span].astype(F32)
        r = qc_refs[c][i, :, span:].astype(F32)
        rows = [jnp.sum((q * q)[h * DH:(h + 1) * DH], axis=0, keepdims=True) for h in range(per_cut)]
        rows += [jnp.sum((q * r)[h * DH:(h + 1) * DH], axis=0, keepdims=True) for h in range(per_cut)]
        if 2 * per_cut < 8:
            rows.append(jnp.zeros((8 - 2 * per_cut, span), F32))
        cols[c, i] = jnp.transpose(jnp.concatenate(rows, axis=0))
        return carry

    sharp_at = dp_tile.at[d]
    sharp_at[...] = jnp.zeros((8, span), F32)
    key_at = lax.broadcasted_iota(jnp.int32, (span, span), 0)
    query_at = lax.broadcasted_iota(jnp.int32, (span, span), 1)
    tail = (lax.broadcasted_iota(jnp.int32, (16, 2 * span), 1) < span).astype(F32).astype(BF16)

    def block(cut, k, carry):
        i = (me + blocks // 2 + k) % blocks
        other = pat_ref[1, i]
        allowed = jnp.concatenate(
            [(i * span + key_at < length) | (key_at == query_at), other * span + key_at < length],
            axis=0)
        for n in range(per_cut):
            h = cut * per_cut + n
            hs = slice(h * DH, (h + 1) * DH)
            ns = slice(n * DH, (n + 1) * DH)
            qc = qc_refs[cut][i, ns, :]
            qc_other = qc_refs[cut][other, ns, :]
            q = qc[:, :span]
            c = qc[:, span:]
            keys = jnp.concatenate([q, qc_other[:, :span]], axis=1)
            key_cots = jnp.concatenate([c, qc_other[:, span:]], axis=1)
            both = dot(keys, qc, 0, 0)
            inner = both[:, :span]
            prob_grad = both[:, span:]
            cross = dot(key_cots, q, 0, 0)
            qf = q.astype(F32)
            cf = c.astype(F32)
            norm_row = jnp.sum(qf * qf, axis=0, keepdims=True)
            pair_row = jnp.sum(qf * cf, axis=0, keepdims=True)
            norm_col = jnp.concatenate([cols[cut, i, :, n:n + 1], cols[cut, other, :, n:n + 1]], axis=0)
            pair_col = jnp.concatenate(
                [cols[cut, i, :, per_cut + n:per_cut + n + 1], cols[cut, other, :, per_cut + n:per_cut + n + 1]],
                axis=0)
            factor = sharp_ref[h] * (1.0 / math.sqrt(DH))
            distance = norm_row + norm_col - 2.0 * inner
            weights = jnp.where(allowed, jnp.exp(-factor * distance), 0.0)
            total = jnp.sum(weights, axis=0, keepdims=True)
            soft = weights * (1.0 / total)
            low = soft.astype(BF16)
            row_inner = jnp.sum(soft * prob_grad, axis=0, keepdims=True)
            score = soft * (prob_grad - row_inner)
            dp_tile[d, h:h + 1, :] += jnp.sum(score * distance, axis=0, keepdims=True)
            coef = (-2.0 * factor * score).astype(BF16)
            row_total = jnp.sum(coef.astype(F32), axis=0, keepdims=True)
            gap = pair_row + pair_col - cross - prob_grad
            gap_mean = jnp.sum(soft * gap, axis=0, keepdims=True)
            adj = (-2.0 * factor * (soft * (gap - gap_mean))).astype(BF16)
            mixed = jnp.concatenate([coef, low], axis=1)
            left = dot(keys, mixed, 1, 0)
            box_a[i, cut, 0, ns, :] = left[:, span:].astype(BF16)
            adjoint = dot(jnp.concatenate([keys, key_cots], axis=1),
                          jnp.concatenate([adj, low], axis=0), 1, 0)
            box_a[i, cut, 1, ns, :] = adjoint.astype(BF16)
            lhs = jnp.concatenate([jnp.concatenate([-q, c], axis=1), tail], axis=0)
            right = dot(lhs, mixed, 1, 1)
            key_part = keys.astype(F32) * right[DH:DH + 1, :] + right[:DH]
            own[i, hs, :] = qf * row_total - left[:, :span] + key_part[:, :span]
            other_part[i, hs, :] = key_part[:, span:]
        pl.when(i != me)(lambda: push_a(i, cut).start())
        for event in events:
            if cut * blocks <= event[0] < (cut + 1) * blocks:
                pl.when(cut * blocks + k == event[0])(functools.partial(run_event, event))
        return carry

    def finish(cut, k, term):
        m = (me + blocks // 2 + k) % blocks
        at = cut_at(cut)

        def gather(i, total):
            chosen = jnp.where(pat_ref[1, i] == m, 1.0, 0.0)
            return total + other_part[i, at] * chosen

        if blocks <= 8:
            g = own[m, at]
            for i in range(blocks):
                g = gather(i, g)
        else:
            g = lax.fori_loop(0, blocks, gather, own[m, at])
        box_g[m, cut] = g.astype(BF16)
        pl.when(m != me)(lambda: push_g(m, cut).start())
        return term + jnp.sum(g * qc_refs[cut][m, :, span:].astype(F32), axis=0, keepdims=True)

    term_one = jnp.zeros((1, span), F32)
    for cut in range(cuts):
        lax.fori_loop(0, blocks, functools.partial(prepare, cut), 0)
        lax.fori_loop(0, blocks, functools.partial(block, cut), 0)
        term_one = lax.fori_loop(0, blocks, functools.partial(finish, cut), term_one)
    for k in range(1, ndp):
        push_d((d + k) % ndp).start()
    home_a[me] = box_a[me]
    home_g[me] = box_g[me]

    for event in events:
        if event[0] >= total_steps:
            run_event(event)

    def whole(t, carry):
        for c in range(cuts):
            complete(line(t) * 2 + 1 - x, c)
        return carry

    lax.fori_loop(0, lines, whole, 0)

    def take_a(k, carry):
        s = (me + k) % blocks
        for c in range(cuts):
            pl.when(k > 0)(lambda: arrived(home_a.at[s, c], a_recv.at[s, c]))
            left_rows[s, :2 * span, cut_at(c)] = jnp.concatenate(
                [jnp.transpose(home_a[s, c, 0]), jnp.transpose(home_a[s, c, 1])], axis=0)
        return carry

    def split(v):
        high = v.astype(BF16).astype(F32)
        mid = (v - high).astype(BF16).astype(F32)
        rows = [high, mid, v - high - mid, jnp.zeros((13, v.shape[1]), F32)]
        return jnp.concatenate(rows, axis=0).astype(BF16)

    start_rows = split(start_ref[...])

    def power(s, total):
        column = jnp.sum(dot(start_rows, w_all[s], 1, 0), axis=0, keepdims=True)
        left_rows[s, 2 * span:, :] = split(column)
        return total + column * column

    column_sq = lax.fori_loop(0, blocks, power, jnp.zeros((1, width), F32))
    lax.fori_loop(0, blocks, take_a, 0)
    step = 256

    def product(rows_ref, r):
        at = pl.ds(pl.multiple_of(r * step, step), step)
        total = jnp.zeros((rows_ref.shape[1], step), F32)
        for s in range(blocks):
            total = total + dot(rows_ref[s], w_all[s, at, :], 1, 1)
        return at, total

    def outward(r, carry):
        at, total = product(left_rows, r)
        branch_ref[:, at] = total[:span].astype(BF16)
        adjoint_out[:, at] = total[span:2 * span]
        image[:, at] = jnp.sum(total[2 * span:], axis=0, keepdims=True)
        return carry

    lax.fori_loop(0, depth // step, outward, 0)

    def take_g(k, carry):
        s = (me + k) % blocks
        for c in range(cuts):
            pl.when(k > 0)(lambda: arrived(home_g.at[s, c], g_recv.at[s, c]))
            grad_rows[s, :, cut_at(c)] = jnp.transpose(home_g[s, c])
        return carry

    lax.fori_loop(0, blocks, take_g, 0)

    def backward(r, term):
        at, total = product(grad_rows, r)
        low = total.astype(BF16)
        vjp_ref[:, at] = low
        part = low.astype(F32) * adjoint_out[:, at]
        for n in range(step // span):
            term = term + jnp.sum(part[:, n * span:(n + 1) * span], axis=0, keepdims=True)
        return term

    image_sq = jnp.sum(image[...] * image[...], axis=1, keepdims=True)
    spec_ref[...] = image[...] / jnp.sqrt(image_sq / depth + 1e-06)
    norm = jnp.sqrt(image_sq / (jnp.sum(column_sq, axis=1, keepdims=True) + 1e-06))
    stat_ref[16:] = jnp.broadcast_to(norm, (8, span))
    term_two = lax.fori_loop(0, depth // step, backward, jnp.zeros((1, span), F32))
    seq_tile[me] = jnp.concatenate([term_one, term_two, jnp.zeros((6, span), F32)], axis=0)
    for k in range(1, blocks):
        push_s((me + k) % blocks).start()
    for k in range(1, ndp):
        j = (d + k) % ndp
        arrived(dp_tile.at[j], d_recv.at[j])
        push_d(j).wait_send()
    for k in range(1, blocks):
        i = (me + k) % blocks
        for c in range(cuts):
            push_a(i, c).wait_send()
            push_g(i, c).wait_send()
        arrived(seq_tile.at[i], s_recv.at[i])
        push_s(i).wait_send()
    push_x().wait_send()
    push_p().wait_send()

    def drain(t, carry):
        at = line(t)
        s = at * 2 + x
        for c in range(cuts):
            pl.when((at <= z) & (z + 1 < lines))(lambda: piece(s, c, d, 0, up, d).wait_send())
            pl.when((at >= z) & (z > 0))(lambda: piece(s, c, d, 1, down, d).wait_send())
            piece(s, c, d, 2, beside, d).wait_send()
            spread_done(at * 2 + 1 - x, c)

        @pl.when(t > 0)
        def _():
            for c in range(cuts):
                spread_done(s, c)
            for c in range(cuts):
                push_q(at, 0, c).wait_send()
                push_q(at, 1, c).wait_send()

        return carry

    lax.fori_loop(0, lines, drain, 0)
    stat_ref[:8] = jnp.broadcast_to(
        jnp.sum(jnp.sum(seq_tile[...], axis=0), axis=1, keepdims=True), (8, span))
    stat_ref[8:16] = jnp.broadcast_to(
        jnp.sum(jnp.sum(dp_tile[...], axis=0), axis=1, keepdims=True), (8, span))


def layer(ndp, groups, tokens, probe_rows, w_query, sharpness, pattern, lengths, start_vector):
    span, depth = tokens.shape
    width = w_query.shape[1]
    blocks, lines = groups, groups // 2
    cuts = max(1, width // 128)
    heads = sharpness.shape[0]
    smem = pl.BlockSpec(memory_space=pltpu.SMEM)
    vmem = pl.BlockSpec(memory_space=pltpu.VMEM)
    hbm = pl.BlockSpec(memory_space=pl.ANY)
    sem = pltpu.SemaphoreType.DMA
    return pl.pallas_call(
        functools.partial(layer_kernel, heads, ndp),
        out_shape=(jax.ShapeDtypeStruct((span, depth), BF16),
                   jax.ShapeDtypeStruct((span, depth), BF16),
                   jax.ShapeDtypeStruct((24, span), F32),
                   jax.ShapeDtypeStruct((1, depth), F32)),
        in_specs=[hbm, hbm, hbm, smem, smem, smem, vmem],
        out_specs=(vmem, vmem, vmem, vmem),
        scratch_shapes=[pltpu.VMEM((2, 2 * span, depth), BF16),
                        pltpu.VMEM((lines, 2, width, 2 * span), BF16),
                        [pltpu.VMEM((blocks, width // cuts, 2 * span), BF16)] * cuts,
                        pltpu.VMEM((1, depth), F32),
                        pltpu.VMEM((cuts, blocks, span, max(8, 2 * heads // cuts)), F32),
                        pltpu.VMEM((blocks, width, span), F32),
                        pltpu.VMEM((blocks, width, span), F32),
                        pltpu.VMEM((blocks, cuts, 2, width // cuts, span), BF16),
                        pltpu.VMEM((blocks, cuts, width // cuts, span), BF16),
                        pltpu.VMEM((blocks, cuts, 2, width // cuts, span), BF16),
                        pltpu.VMEM((blocks, cuts, width // cuts, span), BF16),
                        pltpu.VMEM((blocks, 2 * span + 16, width), BF16),
                        pltpu.VMEM((blocks, span, width), BF16),
                        pltpu.VMEM((span, depth), F32),
                        pltpu.VMEM((blocks, depth, width), BF16),
                        pltpu.VMEM((blocks, 8, span), F32),
                        pltpu.VMEM((ndp, 8, span), F32),
                        sem((3,)), sem((2,)), sem((2,)), sem((2 + ndp, blocks * cuts)), sem((ndp, blocks * cuts)),
                        sem((lines, 2, cuts)), sem((blocks, cuts)), sem((blocks, cuts)), sem((blocks, cuts)),
                        sem((blocks, cuts)), sem((blocks, cuts)), sem((blocks,)), sem((blocks,)), sem((ndp,)),
                        sem((ndp,))],
        compiler_params=pltpu.CompilerParams(collective_id=0, has_side_effects=True,
                                             vmem_limit_bytes=56 * 1024 * 1024),
        name="layer",
    )(tokens, probe_rows, w_query, sharpness, pattern, lengths, start_vector.reshape(1, depth))


def keep_kernel(scale_term, scale_sharp, a_ref, b_ref, stat_ref, spec_ref, len_ref, a_out, b_out, term_out,
                sharp_out, spec_out, norm_out):
    a_out[...] = a_ref[...]
    b_out[...] = b_ref[...]
    spec_out[...] = spec_ref[...]
    span = stat_ref.shape[1]
    row_at = lax.broadcasted_iota(jnp.int32, (8, span), 0)
    column_at = lax.broadcasted_iota(jnp.int32, (8, span), 1)

    def as_row(at):
        return jnp.sum(jnp.where(row_at == column_at, stat_ref[at:at + 8], 0.0), axis=0, keepdims=True)

    count = jnp.full((1, span), len_ref[0], jnp.int32).astype(F32) * scale_term
    term_out[...] = (as_row(0) / count)[:, :term_out.shape[1]]
    sharp_out[...] = (as_row(8) * scale_sharp)[:, :sharp_out.shape[1]]
    norm_out[...] = stat_ref[16:17, :1]


def keep(a, b, stats, spec, lengths, heads, scale_term, scale_sharp):
    smem = pl.BlockSpec(memory_space=pltpu.SMEM)
    vmem = pl.BlockSpec(memory_space=pltpu.VMEM)
    return pl.pallas_call(
        functools.partial(keep_kernel, scale_term, scale_sharp),
        out_shape=(jax.ShapeDtypeStruct(a.shape, a.dtype), jax.ShapeDtypeStruct(b.shape, b.dtype),
                   jax.ShapeDtypeStruct((1, 2), F32), jax.ShapeDtypeStruct((1, heads), F32),
                   jax.ShapeDtypeStruct(spec.shape, F32), jax.ShapeDtypeStruct((1, 1), F32)),
        in_specs=[vmem, vmem, vmem, vmem, smem],
        out_specs=(vmem,) * 6, name="keep")(a, b, stats, spec, lengths)


def shards(inputs, w_query, sharpness, pattern, lengths, probes, start_vector):
    tokens = inputs[0]
    probe_rows = probes[0]
    rows_here = tokens.shape[0]
    groups = lax.axis_size("seq")
    inner_here = w_query.shape[1]
    inner = inner_here * groups
    branch, probe_vjp, stats, spec = layer(
        lax.axis_size("dp"), groups, tokens, probe_rows, w_query, sharpness, pattern.T, lengths, start_vector)
    heads = sharpness.shape[0]
    scale_sharp = -1.0 / math.sqrt(DH) / (lax.axis_size("dp") * groups * rows_here * DH)
    branch, probe_vjp, terms, sharp_grad, spec, norm = keep(
        branch, probe_vjp, stats, spec, lengths, heads, float(inner), scale_sharp)
    return (branch[None], probe_vjp[None], terms, sharp_grad.reshape(-1), spec.reshape(-1), norm.reshape(-1))


def solution(mesh):
    placed = (
        P("dp", "seq", None),
        P(None, "seq"),
        P("seq"),
        P(),
        P("dp"),
        P("dp", "seq", None),
        P(),
    )
    return jax.shard_map(
        shards,
        mesh=mesh,
        in_specs=placed,
        out_specs=(P("dp", "seq", None), P("dp", "seq", None), P("dp", None), P("seq"), P(), P()),
        check_vma=False,
    )
```

```python
import functools
import math

import jax
import jax.numpy as jnp
from jax import lax
from jax.experimental import pallas as pl
from jax.experimental.pallas import tpu as pltpu
from jax.sharding import PartitionSpec as P

DH = 64
F32 = jnp.float32
BF16 = jnp.bfloat16


def dot(a, b, ca, cb):
    return lax.dot_general(a, b, (((ca,), (cb,)), ((), ())), preferred_element_type=F32)


def layer_kernel(heads, ndp, x_ref, p_ref, w_ref, sharp_ref, pat_ref, len_ref, start_ref, branch_out,
                 vjp_out, stat_ref, spec_ref, branch_ref, vjp_ref, out_sem, both, outbox, qc_refs, image, cols, own, other_part, box_a, box_g,
                 home_a, home_g, left_rows, grad_rows, adjoint_out, w_all, seq_tile, dp_tile, loc_sem, x_send,
                 x_recv, w_send, w_recv, q_send, q_recv, a_send, a_recv, g_send, g_recv, s_send, s_recv, d_send,
                 d_recv):
    blocks, depth, width = w_all.shape
    pair = both.shape[1]
    span = pair // 2
    lines, ys, rows = blocks // 2, ndp // 2, depth // ndp
    cuts = max(1, width // 128)
    part_width = width // cuts
    me, d = lax.axis_index("seq"), lax.axis_index("dp")
    z, x = me // 2, me % 2
    y, core = d // 2, d % 2
    mate_d = d + 1 - 2 * core
    beside = me + 1 - 2 * x
    length = len_ref[0]
    mesh_id = pl.DeviceIdType.MESH

    loads = [pltpu.make_async_copy(w_ref, w_all.at[me], loc_sem.at[0]),
             pltpu.make_async_copy(x_ref, both.at[x, :span], loc_sem.at[1]),
             pltpu.make_async_copy(p_ref, both.at[x, span:], loc_sem.at[2])]
    for load in loads:
        load.start()
    barrier = pltpu.get_barrier_semaphore()
    for k in range(1, blocks):
        pl.semaphore_signal(barrier, inc=1, device_id={"seq": (me + k) % blocks, "dp": d},
                            device_id_type=mesh_id)
    for k in range(1, ndp):
        pl.semaphore_signal(barrier, inc=1, device_id={"seq": me, "dp": (d + k) % ndp},
                            device_id_type=mesh_id)
    pl.semaphore_wait(barrier, blocks + ndp - 2)

    def push(src, dst, send, recv, target, t_dp):
        return pltpu.make_async_remote_copy(
            src_ref=src, dst_ref=dst, send_sem=send, recv_sem=recv,
            device_id={"seq": target, "dp": t_dp}, device_id_type=mesh_id)

    def push_a(i, c):
        return push(box_a.at[i, c], home_a.at[me, c], a_send.at[i, c], a_recv.at[me, c], i, d)

    def push_g(i, c):
        return push(box_g.at[i, c], home_g.at[me, c], g_send.at[i, c], g_recv.at[me, c], i, d)

    def push_s(i):
        return push(seq_tile.at[me], seq_tile.at[me], s_send.at[i], s_recv.at[me], i, d)

    def push_d(j):
        return push(dp_tile.at[d], dp_tile.at[d], d_send.at[j], d_recv.at[d], me, j)

    def arrived(ref, sem):
        pltpu.make_async_copy(ref, ref, sem).wait()

    def push_x():
        return push(x_ref, both.at[x, :span], x_send.at[0], x_recv.at[0], beside, d)

    def push_p():
        return push(p_ref, both.at[x, span:], x_send.at[1], x_recv.at[1], beside, d)

    def part(owner):
        return pl.ds(pl.multiple_of(owner * rows, rows), rows)

    def cut_at(c):
        return slice(c * part_width, (c + 1) * part_width)

    def piece(s, c, owner, kind, target, t_dp, first=False):
        here = w_all.at[s, part(owner), cut_at(c)]
        src = w_ref.at[part(owner), cut_at(c)] if first else here
        at = s * cuts + c
        return push(src, here, w_send.at[kind, at], w_recv.at[owner, at], target, t_dp)

    def landed(s, c, owner):
        arrived(w_all.at[s, part(owner), cut_at(c)], w_recv.at[owner, s * cuts + c])

    up, down = (me + 2) % blocks, (me + blocks - 2) % blocks

    def line(t):
        m = jnp.minimum(z, lines - 1 - z)
        near = jnp.where(t % 2 == 1, z + (t + 1) // 2, z - t // 2)
        far = jnp.where(2 * z < lines, t, lines - 1 - t)
        return jnp.where(t <= 2 * m, near, far)

    def spread(s, c):
        for k in range(1, ys):
            piece(s, c, d, 3 + k, me, ((y + k) % ys) * 2 + core).start()
        piece(s, c, d, 3, me, mate_d).start()

    def relay(s, c):
        for k in range(1, ys):
            owner = ((y + k) % ys) * 2 + core
            landed(s, c, owner)
            piece(s, c, owner, 2 + ys + k, me, mate_d).start()

    def complete(s, c):
        for k in range(ys):
            landed(s, c, ((y + k) % ys) * 2 + 1 - core)

    def spread_done(s, c):
        for k in range(1, ys):
            piece(s, c, d, 3 + k, me, d).wait_send()
            piece(s, c, d, 2 + ys + k, me, d).wait_send()
        piece(s, c, d, 3, me, d).wait_send()

    def forward(t, c):
        at = line(t)
        s = at * 2 + x
        landed(s, c, d)
        pl.when((at < z) & (z + 1 < lines))(lambda: piece(s, c, d, 0, up, d).start())
        pl.when((at > z) & (z > 0))(lambda: piece(s, c, d, 1, down, d).start())
        spread(s, c)
        piece(s, c, d, 2, beside, d).start()

    def own_piece(c):
        pl.when(z + 1 < lines)(lambda: piece(me, c, d, 0, up, d, True).start())
        pl.when(z > 0)(lambda: piece(me, c, d, 1, down, d, True).start())

    own_piece(0)
    push_x().start()
    push_p().start()
    for c in range(cuts):
        piece(me, c, d, 2, beside, d, True).start()
    token_at = lax.broadcasted_iota(jnp.int32, (1, span), 1)

    def project(s, side, c):
        res = jnp.transpose(dot(both[side], w_all[s, :, cut_at(c)], 1, 0))
        kept = jnp.concatenate([token_at >= 0, (z * 2 + side) * span + token_at < length], axis=1)
        return jnp.where(kept, res, 0.0).astype(BF16)

    def push_q(at, side, c):
        block_at = z * 2 + side
        return push(outbox.at[at, side, cut_at(c)], qc_refs[c].at[block_at], q_send.at[at, side, c],
                    q_recv.at[block_at, c], at * 2 + x, d)

    for load in loads:
        load.wait()
    for c in range(cuts):
        qc_refs[c][me] = project(me, x, c)

    def first_product(t, c):
        at = line(t)
        s = at * 2 + x
        relay(s, c)
        complete(s, c)
        outbox[at, x, cut_at(c)] = project(s, x, c)
        push_q(at, x, c).start()

    lag = jnp.where((z > 0) & (z + 1 < lines), 2, 1)
    for c in range(cuts):

        def tick(t, carry):
            forward(t, c)
            if c + 1 < cuts:
                pl.when(t == jnp.minimum(lag, 2))(lambda: own_piece(c + 1))
            pl.when(t > lag)(lambda: first_product(t - lag, c))
            if c > 0:
                pl.when((t <= lag) & (t + lines - 1 > lag))(lambda: first_product(t + lines - 1 - lag, c - 1))
            return carry

        lax.fori_loop(1, lines, tick, 0)

    def rest(t, carry):
        pl.when(t + lag >= lines)(lambda: first_product(t, cuts - 1))
        return carry

    lax.fori_loop(1, lines, rest, 0)

    arrived(both.at[1 - x, :span], x_recv.at[0])
    arrived(both.at[1 - x, span:], x_recv.at[1])
    for c in range(cuts):

        def partner(t, carry):
            at = line(t)
            outbox[at, 1 - x, cut_at(c)] = project(at * 2 + x, 1 - x, c)
            push_q(at, 1 - x, c).start()
            return carry

        lax.fori_loop(1, lines, partner, 0)
        qc_refs[c][beside] = project(me, 1 - x, c)

    units = [(0, c) for c in range(cuts)] + [(t, c) for c in range(cuts) for t in range(1, lines)]

    def spread_other(g):
        for t, c in units[g * cuts:(g + 1) * cuts]:
            s = line(t) * 2 + 1 - x
            landed(s, c, d)
            spread(s, c)

    def relay_other(g):
        for t, c in units[g * cuts:(g + 1) * cuts]:
            relay(line(t) * 2 + 1 - x, c)

    total_steps = cuts * blocks
    stride = max(1, (total_steps - 2) // max(1, lines - 2))
    events = [(4 + stride * (g - 2), 0, g) for g in range(2, lines)]
    events += [(5 + (stride + 1) * (g - 1), 1, g) for g in range(1, lines)]
    events.sort()

    def run_event(event):
        (relay_other if event[1] else spread_other)(event[2])

    spread_other(0)
    spread_other(1)
    relay_other(0)
    per_cut = heads // cuts

    def prepare(c, k, carry):
        i = (me - x + k) % blocks
        pl.when(k > 1)(lambda: arrived(qc_refs[c].at[i], q_recv.at[i, c]))
        q = qc_refs[c][i, :, :span].astype(F32)
        r = qc_refs[c][i, :, span:].astype(F32)
        rows = [jnp.sum((q * q)[h * DH:(h + 1) * DH], axis=0, keepdims=True) for h in range(per_cut)]
        rows += [jnp.sum((q * r)[h * DH:(h + 1) * DH], axis=0, keepdims=True) for h in range(per_cut)]
        if 2 * per_cut < 8:
            rows.append(jnp.zeros((8 - 2 * per_cut, span), F32))
        cols[c, i] = jnp.transpose(jnp.concatenate(rows, axis=0))
        return carry

    sharp_at = dp_tile.at[d]
    sharp_at[...] = jnp.zeros((8, span), F32)
    key_at = lax.broadcasted_iota(jnp.int32, (span, span), 0)
    query_at = lax.broadcasted_iota(jnp.int32, (span, span), 1)
    tail = (lax.broadcasted_iota(jnp.int32, (16, 2 * span), 1) < span).astype(F32).astype(BF16)

    def block(cut, k, carry):
        i = (me + blocks // 2 + k) % blocks
        other = pat_ref[1, i]
        allowed = jnp.concatenate(
            [(i * span + key_at < length) | (key_at == query_at), other * span + key_at < length],
            axis=0)
        for n in range(per_cut):
            h = cut * per_cut + n
            hs = slice(h * DH, (h + 1) * DH)
            ns = slice(n * DH, (n + 1) * DH)
            qc = qc_refs[cut][i, ns, :]
            qc_other = qc_refs[cut][other, ns, :]
            q = qc[:, :span]
            c = qc[:, span:]
            keys = jnp.concatenate([q, qc_other[:, :span]], axis=1)
            key_cots = jnp.concatenate([c, qc_other[:, span:]], axis=1)
            both = dot(keys, qc, 0, 0)
            inner = both[:, :span]
            prob_grad = both[:, span:]
            cross = dot(key_cots, q, 0, 0)
            qf = q.astype(F32)
            cf = c.astype(F32)
            norm_row = jnp.sum(qf * qf, axis=0, keepdims=True)
            pair_row = jnp.sum(qf * cf, axis=0, keepdims=True)
            norm_col = jnp.concatenate([cols[cut, i, :, n:n + 1], cols[cut, other, :, n:n + 1]], axis=0)
            pair_col = jnp.concatenate(
                [cols[cut, i, :, per_cut + n:per_cut + n + 1], cols[cut, other, :, per_cut + n:per_cut + n + 1]],
                axis=0)
            factor = sharp_ref[h] * (1.0 / math.sqrt(DH))
            distance = norm_row + norm_col - 2.0 * inner
            weights = jnp.where(allowed, jnp.exp(-factor * distance), 0.0)
            total = jnp.sum(weights, axis=0, keepdims=True)
            soft = weights * (1.0 / total)
            low = soft.astype(BF16)
            row_inner = jnp.sum(soft * prob_grad, axis=0, keepdims=True)
            score = soft * (prob_grad - row_inner)
            dp_tile[d, h:h + 1, :] += jnp.sum(score * distance, axis=0, keepdims=True)
            coef = (-2.0 * factor * score).astype(BF16)
            row_total = jnp.sum(coef.astype(F32), axis=0, keepdims=True)
            gap = pair_row + pair_col - cross - prob_grad
            gap_mean = jnp.sum(soft * gap, axis=0, keepdims=True)
            adj = (-2.0 * factor * (soft * (gap - gap_mean))).astype(BF16)
            mixed = jnp.concatenate([coef, low], axis=1)
            left = dot(keys, mixed, 1, 0)
            box_a[i, cut, 0, ns, :] = left[:, span:].astype(BF16)
            adjoint = dot(jnp.concatenate([keys, key_cots], axis=1),
                          jnp.concatenate([adj, low], axis=0), 1, 0)
            box_a[i, cut, 1, ns, :] = adjoint.astype(BF16)
            lhs = jnp.concatenate([jnp.concatenate([-q, c], axis=1), tail], axis=0)
            right = dot(lhs, mixed, 1, 1)
            key_part = keys.astype(F32) * right[DH:DH + 1, :] + right[:DH]
            own[i, hs, :] = qf * row_total - left[:, :span] + key_part[:, :span]
            other_part[i, hs, :] = key_part[:, span:]
        pl.when(i != me)(lambda: push_a(i, cut).start())
        for event in events:
            if cut * blocks <= event[0] < (cut + 1) * blocks:
                pl.when(cut * blocks + k == event[0])(functools.partial(run_event, event))
        return carry

    def finish(cut, k, term):
        m = (me + blocks // 2 + k) % blocks
        at = cut_at(cut)

        def gather(i, total):
            chosen = jnp.where(pat_ref[1, i] == m, 1.0, 0.0)
            return total + other_part[i, at] * chosen

        if blocks <= 8:
            g = own[m, at]
            for i in range(blocks):
                g = gather(i, g)
        else:
            g = lax.fori_loop(0, blocks, gather, own[m, at])
        box_g[m, cut] = g.astype(BF16)
        pl.when(m != me)(lambda: push_g(m, cut).start())
        return term + jnp.sum(g * qc_refs[cut][m, :, span:].astype(F32), axis=0, keepdims=True)

    term_one = jnp.zeros((1, span), F32)
    for cut in range(cuts):
        lax.fori_loop(0, blocks, functools.partial(prepare, cut), 0)
        lax.fori_loop(0, blocks, functools.partial(block, cut), 0)
        term_one = lax.fori_loop(0, blocks, functools.partial(finish, cut), term_one)
    for k in range(1, ndp):
        push_d((d + k) % ndp).start()
    home_a[me] = box_a[me]
    home_g[me] = box_g[me]

    for event in events:
        if event[0] >= total_steps:
            run_event(event)

    def whole(t, carry):
        for c in range(cuts):
            complete(line(t) * 2 + 1 - x, c)
        return carry

    lax.fori_loop(0, lines, whole, 0)

    def take_a(k, carry):
        s = (me + k) % blocks
        for c in range(cuts):
            pl.when(k > 0)(lambda: arrived(home_a.at[s, c], a_recv.at[s, c]))
            left_rows[s, :2 * span, cut_at(c)] = jnp.concatenate(
                [jnp.transpose(home_a[s, c, 0]), jnp.transpose(home_a[s, c, 1])], axis=0)
        return carry

    def split(v):
        high = v.astype(BF16).astype(F32)
        mid = (v - high).astype(BF16).astype(F32)
        rows = [high, mid, v - high - mid, jnp.zeros((13, v.shape[1]), F32)]
        return jnp.concatenate(rows, axis=0).astype(BF16)

    start_rows = split(start_ref[...])

    def power(s, total):
        column = jnp.sum(dot(start_rows, w_all[s], 1, 0), axis=0, keepdims=True)
        left_rows[s, 2 * span:, :] = split(column)
        return total + column * column

    column_sq = lax.fori_loop(0, blocks, power, jnp.zeros((1, width), F32))
    lax.fori_loop(0, blocks, take_a, 0)
    step = 256

    def product(rows_ref, r):
        at = pl.ds(pl.multiple_of(r * step, step), step)
        total = jnp.zeros((rows_ref.shape[1], step), F32)
        for s in range(blocks):
            total = total + dot(rows_ref[s], w_all[s, at, :], 1, 1)
        return at, total

    def outward(r, carry):
        at, total = product(left_rows, r)
        branch_ref[:, at] = total[:span].astype(BF16)
        adjoint_out[:, at] = total[span:2 * span]
        image[:, at] = jnp.sum(total[2 * span:], axis=0, keepdims=True)
        return carry

    lax.fori_loop(0, depth // step, outward, 0)
    save_branch = pltpu.make_async_copy(branch_ref, branch_out, out_sem.at[0])
    save_branch.start()

    def take_g(k, carry):
        s = (me + k) % blocks
        for c in range(cuts):
            pl.when(k > 0)(lambda: arrived(home_g.at[s, c], g_recv.at[s, c]))
            grad_rows[s, :, cut_at(c)] = jnp.transpose(home_g[s, c])
        return carry

    lax.fori_loop(0, blocks, take_g, 0)

    def backward(r, term):
        at, total = product(grad_rows, r)
        low = total.astype(BF16)
        vjp_ref[:, at] = low
        part = low.astype(F32) * adjoint_out[:, at]
        for n in range(step // span):
            term = term + jnp.sum(part[:, n * span:(n + 1) * span], axis=0, keepdims=True)
        return term

    image_sq = jnp.sum(image[...] * image[...], axis=1, keepdims=True)
    spec_ref[...] = image[...] / jnp.sqrt(image_sq / depth + 1e-06)
    norm = jnp.sqrt(image_sq / (jnp.sum(column_sq, axis=1, keepdims=True) + 1e-06))
    stat_ref[16:] = jnp.broadcast_to(norm, (8, span))
    term_two = lax.fori_loop(0, depth // step, backward, jnp.zeros((1, span), F32))
    seq_tile[me] = jnp.concatenate([term_one, term_two, jnp.zeros((6, span), F32)], axis=0)
    for k in range(1, blocks):
        push_s((me + k) % blocks).start()
    save_vjp = pltpu.make_async_copy(vjp_ref, vjp_out, out_sem.at[1])
    save_vjp.start()
    for k in range(1, ndp):
        j = (d + k) % ndp
        arrived(dp_tile.at[j], d_recv.at[j])
        push_d(j).wait_send()
    for k in range(1, blocks):
        i = (me + k) % blocks
        for c in range(cuts):
            push_a(i, c).wait_send()
            push_g(i, c).wait_send()
        arrived(seq_tile.at[i], s_recv.at[i])
        push_s(i).wait_send()
    push_x().wait_send()
    push_p().wait_send()
    save_branch.wait()
    save_vjp.wait()

    def drain(t, carry):
        at = line(t)
        s = at * 2 + x
        for c in range(cuts):
            pl.when((at <= z) & (z + 1 < lines))(lambda: piece(s, c, d, 0, up, d).wait_send())
            pl.when((at >= z) & (z > 0))(lambda: piece(s, c, d, 1, down, d).wait_send())
            piece(s, c, d, 2, beside, d).wait_send()
            spread_done(at * 2 + 1 - x, c)

        @pl.when(t > 0)
        def _():
            for c in range(cuts):
                spread_done(s, c)
            for c in range(cuts):
                push_q(at, 0, c).wait_send()
                push_q(at, 1, c).wait_send()

        return carry

    lax.fori_loop(0, lines, drain, 0)
    stat_ref[:8] = jnp.broadcast_to(
        jnp.sum(jnp.sum(seq_tile[...], axis=0), axis=1, keepdims=True), (8, span))
    stat_ref[8:16] = jnp.broadcast_to(
        jnp.sum(jnp.sum(dp_tile[...], axis=0), axis=1, keepdims=True), (8, span))


def layer(ndp, groups, tokens, probe_rows, w_query, sharpness, pattern, lengths, start_vector):
    span, depth = tokens.shape
    width = w_query.shape[1]
    blocks, lines = groups, groups // 2
    cuts = max(1, width // 128)
    heads = sharpness.shape[0]
    smem = pl.BlockSpec(memory_space=pltpu.SMEM)
    vmem = pl.BlockSpec(memory_space=pltpu.VMEM)
    hbm = pl.BlockSpec(memory_space=pl.ANY)
    sem = pltpu.SemaphoreType.DMA
    return pl.pallas_call(
        functools.partial(layer_kernel, heads, ndp),
        out_shape=(jax.ShapeDtypeStruct((span, depth), BF16),
                   jax.ShapeDtypeStruct((span, depth), BF16),
                   jax.ShapeDtypeStruct((24, span), F32),
                   jax.ShapeDtypeStruct((1, depth), F32)),
        in_specs=[hbm, hbm, hbm, smem, smem, smem, vmem],
        out_specs=(hbm, hbm, vmem, vmem),
        scratch_shapes=[pltpu.VMEM((span, depth), BF16),
                        pltpu.VMEM((span, depth), BF16),
                        sem((2,)),
                        pltpu.VMEM((2, 2 * span, depth), BF16),
                        pltpu.VMEM((lines, 2, width, 2 * span), BF16),
                        [pltpu.VMEM((blocks, width // cuts, 2 * span), BF16)] * cuts,
                        pltpu.VMEM((1, depth), F32),
                        pltpu.VMEM((cuts, blocks, span, max(8, 2 * heads // cuts)), F32),
                        pltpu.VMEM((blocks, width, span), F32),
                        pltpu.VMEM((blocks, width, span), F32),
                        pltpu.VMEM((blocks, cuts, 2, width // cuts, span), BF16),
                        pltpu.VMEM((blocks, cuts, width // cuts, span), BF16),
                        pltpu.VMEM((blocks, cuts, 2, width // cuts, span), BF16),
                        pltpu.VMEM((blocks, cuts, width // cuts, span), BF16),
                        pltpu.VMEM((blocks, 2 * span + 16, width), BF16),
                        pltpu.VMEM((blocks, span, width), BF16),
                        pltpu.VMEM((span, depth), F32),
                        pltpu.VMEM((blocks, depth, width), BF16),
                        pltpu.VMEM((blocks, 8, span), F32),
                        pltpu.VMEM((ndp, 8, span), F32),
                        sem((3,)), sem((2,)), sem((2,)), sem((2 + ndp, blocks * cuts)), sem((ndp, blocks * cuts)),
                        sem((lines, 2, cuts)), sem((blocks, cuts)), sem((blocks, cuts)), sem((blocks, cuts)),
                        sem((blocks, cuts)), sem((blocks, cuts)), sem((blocks,)), sem((blocks,)), sem((ndp,)),
                        sem((ndp,))],
        compiler_params=pltpu.CompilerParams(collective_id=0, has_side_effects=True,
                                             vmem_limit_bytes=56 * 1024 * 1024),
        name="layer",
    )(tokens, probe_rows, w_query, sharpness, pattern, lengths, start_vector.reshape(1, depth))


def keep_kernel(scale_term, scale_sharp, a_ref, b_ref, stat_ref, spec_ref, len_ref, a_out, b_out, term_out,
                sharp_out, spec_out, norm_out):
    a_out[...] = a_ref[...]
    b_out[...] = b_ref[...]
    spec_out[...] = spec_ref[...]
    span = stat_ref.shape[1]
    row_at = lax.broadcasted_iota(jnp.int32, (8, span), 0)
    column_at = lax.broadcasted_iota(jnp.int32, (8, span), 1)

    def as_row(at):
        return jnp.sum(jnp.where(row_at == column_at, stat_ref[at:at + 8], 0.0), axis=0, keepdims=True)

    count = jnp.full((1, span), len_ref[0], jnp.int32).astype(F32) * scale_term
    term_out[...] = (as_row(0) / count)[:, :term_out.shape[1]]
    sharp_out[...] = (as_row(8) * scale_sharp)[:, :sharp_out.shape[1]]
    norm_out[...] = stat_ref[16:17, :1]


def keep(a, b, stats, spec, lengths, heads, scale_term, scale_sharp):
    smem = pl.BlockSpec(memory_space=pltpu.SMEM)
    vmem = pl.BlockSpec(memory_space=pltpu.VMEM)
    return pl.pallas_call(
        functools.partial(keep_kernel, scale_term, scale_sharp),
        out_shape=(jax.ShapeDtypeStruct(a.shape, a.dtype), jax.ShapeDtypeStruct(b.shape, b.dtype),
                   jax.ShapeDtypeStruct((1, 2), F32), jax.ShapeDtypeStruct((1, heads), F32),
                   jax.ShapeDtypeStruct(spec.shape, F32), jax.ShapeDtypeStruct((1, 1), F32)),
        in_specs=[vmem, vmem, vmem, vmem, smem],
        out_specs=(vmem,) * 6, name="keep")(a, b, stats, spec, lengths)


def shards(inputs, w_query, sharpness, pattern, lengths, probes, start_vector):
    tokens = inputs[0]
    probe_rows = probes[0]
    rows_here = tokens.shape[0]
    groups = lax.axis_size("seq")
    inner_here = w_query.shape[1]
    inner = inner_here * groups
    branch, probe_vjp, stats, spec = layer(
        lax.axis_size("dp"), groups, tokens, probe_rows, w_query, sharpness, pattern.T, lengths, start_vector)
    heads = sharpness.shape[0]
    scale_sharp = -1.0 / math.sqrt(DH) / (lax.axis_size("dp") * groups * rows_here * DH)
    branch, probe_vjp, terms, sharp_grad, spec, norm = keep(
        branch, probe_vjp, stats, spec, lengths, heads, float(inner), scale_sharp)
    return (branch[None], probe_vjp[None], terms, sharp_grad.reshape(-1), spec.reshape(-1), norm.reshape(-1))


def solution(mesh):
    placed = (
        P("dp", "seq", None),
        P(None, "seq"),
        P("seq"),
        P(),
        P("dp"),
        P("dp", "seq", None),
        P(),
    )
    return jax.shard_map(
        shards,
        mesh=mesh,
        in_specs=placed,
        out_specs=(P("dp", "seq", None), P("dp", "seq", None), P("dp", None), P("seq"), P(), P()),
        check_vma=False,
    )
```
